32 devices in a mesh: half: 2 (over y), gx: 4 (over x, core), yz: 4 (over z).
Axes of the slice: x: 2, y: 2, z: 4, core: 2. Of those that a mesh axis runs over, the one named last changes fastest.
Arguments:
- fields: float32 [2, 256, 256, 128], P('half', 'gx', 'yz'), may hold values from -6 to 6
- forcing: float32 [256, 256, 128], P('gx', 'yz'), may hold values from -6 to 6
- step_index: int32 [1], replicated, may hold values from 0 to 63
Outputs:
- fields_out: float32 [2, 256, 256, 128], P('half', 'gx', 'yz')
The draws below stay inside these ranges and needn't reach their ends.
All inputs are finite; a program needn't handle non-finite values.
Results may differ from the reference program's by a relative error of at most 0.0001.
Values sent between devices are 32-bit elements; how exact they have to be, the bound alone decides.
A program may use at most 128 MiB of HBM per device.

```python
import math
import jax
import jax.numpy as jnp

NZ = 128
ITERS = 4
NX = 256
NY = 256


def block_scale(own_key, shape, split, least, high):
    def one(dim, shards_of):
        steps = jax.random.uniform(jax.random.fold_in(jax.random.fold_in(own_key, 6), dim), (shards_of,), jnp.float32, least / len(split), high / len(split))
        return jnp.repeat(jnp.exp(steps), shape[dim] // shards_of).reshape((-1,) + (1,) * (len(shape) - dim - 1))

    factor_of = one(*split[0])
    for cut in split[1:]:
        factor_of = factor_of * one(*cut)
    return factor_of


def normal_values(rng, extent, spread, most, split=(), kind=jnp.bfloat16):
    level = block_scale(rng, extent, split, -0.22, 0.18) if split else 1.0
    drawn = jax.random.normal(rng, extent, jnp.float32) * spread * level
    return jnp.minimum(jnp.maximum(drawn, -most), most).astype(kind)


def setup_inputs(seed: int = 0) -> dict:
    splits = jax.random.split(jax.random.key(seed), 4)
    fields = normal_values(splits[0], (2, NX, NY, NZ), 1.0, 6.0, ((0, 2), (1, 4), (2, 4)), jnp.float32)
    forcing = normal_values(splits[1], (NX, NY, NZ), 1.0, 6.0, ((0, 4), (1, 4)), jnp.float32)
    step_index = jax.random.randint(splits[2], (1,), 0, 64).astype(jnp.int32)
    return dict(fields=fields, forcing=forcing, step_index=step_index)


def inner(padded):
    return padded[1:-1, 1:-1, 1:-1]

def along_x(padded):
    return 0.5 * (padded[2:, 1:-1, 1:-1] - padded[:-2, 1:-1, 1:-1])

def laplace(padded):
    total = padded[2:, 1:-1, 1:-1] + padded[:-2, 1:-1, 1:-1]
    total = total + padded[1:-1, 2:, 1:-1] + padded[1:-1, :-2, 1:-1]
    total = total + padded[1:-1, 1:-1, 2:] + padded[1:-1, 1:-1, :-2]
    return total - 6.0 * inner(padded)

def advance(field, forcing, phase):
    padded = jnp.pad(field, 1)
    return field + 0.2 * (-field * along_x(padded) + 0.5 * laplace(padded) + forcing * jnp.sin(phase))

def reference(fields, forcing, step_index):
    omega = 2.0 * math.pi / 64.0
    state = fields[0]
    states = []
    phases = []
    for step in range(ITERS):
        phase = (step_index[0] + step).astype(jnp.float32) * omega
        states.append(state)
        phases.append(phase)
        state = advance(state, forcing, phase)
    adjoint = fields[1]
    for step in reversed(range(ITERS)):
        phase = phases[step]
        _, pullback = jax.vjp(lambda field: advance(field, forcing, phase), states[step])
        adjoint = pullback(adjoint)[0]
    return jnp.stack([state, adjoint])
```

```python
import functools
import math

import jax
import jax.numpy as jnp
from jax import lax
from jax.experimental import pallas as pl
from jax.experimental.pallas import tpu as pltpu
from jax.sharding import PartitionSpec as P

ITERS = 4
MESH = pl.DeviceIdType.MESH


def window(W, step_ref, fields, forcing, out, state, yh, sy, force, level, xs, xr, ys, yr, fs, fr, local, go):
    X, Y, Z = forcing.shape
    n = X // W
    M = W + 1
    hold = 2 * ITERS
    side = lax.axis_index("half")
    gx, nx = lax.axis_index("gx"), lax.axis_size("gx")
    gy, ny = lax.axis_index("yz"), lax.axis_size("yz")

    flip = lax.rem(gx, 2)
    home = lax.rem(lax.div(gx + 1, 2), 2)
    full = jnp.where(side == 1, home, 1 - home)
    base_side = side == 0
    is_full, is_home = full == 1, home == 1
    works = jnp.logical_or(base_side, is_full)
    away_full = jnp.logical_and(base_side, is_full)
    home_full = jnp.logical_and(side == 1, is_full)
    base_only = jnp.logical_and(base_side, is_home)
    idle = jnp.logical_and(side == 1, home == 0)

    has_far = jnp.logical_or(jnp.logical_and(flip == 0, gx > 0), jnp.logical_and(flip == 1, gx < nx - 1))
    has_down, has_up = gy > 0, gy < ny - 1
    far = {"gx": lax.rem(gx + nx - 1 + 2 * flip, nx)}
    mate = {"gx": gx + 1 - 2 * flip}
    down, up = {"yz": lax.rem(gy + ny - 1, ny)}, {"yz": lax.rem(gy + 1, ny)}
    other = {"half": 1 - side}
    across = {"half": 1 - side, "gx": gx + 1 - 2 * flip}

    def first(p):
        return p * W + flip * (X - (2 * p + 1) * W)

    def remote(src, dst, s, r, dev):
        return pltpu.make_async_remote_copy(
            src_ref=src, dst_ref=dst, send_sem=s, recv_sem=r, device_id=dev, device_id_type=MESH
        )

    def x_far(k):
        src, dst = M + flip * (X - 1), M + X - flip * (X + 1)
        return remote(state.at[k, src], state.at[k, dst], xs.at[k], xr.at[k], far)

    def y_down(k, p):
        part = pl.ds(pl.multiple_of(W + first(p), W), W)
        return remote(sy.at[k, 0, part], yh.at[k, 1, part], ys.at[k, 0, p], yr.at[k, 0, p], down)

    def y_up(k, p):
        part = pl.ds(pl.multiple_of(W + first(p), W), W)
        return remote(sy.at[k, 1, part], yh.at[k, 0, part], ys.at[k, 1, p], yr.at[k, 1, p], up)

    def brick(p):
        src, dst = fields.at[0, pl.ds(first(p), W)], state.at[0, pl.ds(M + first(p), W)]
        return remote(src, dst, fs.at[0, p], fr.at[0, p], other)

    def lent(p):
        src, dst = fields.at[0, pl.ds(first(p), W)], state.at[ITERS, pl.ds(M + first(p), W)]
        return remote(src, dst, fs.at[1, p], fr.at[1, p], other)

    def returned(p):
        src, dst = state.at[2 * ITERS, pl.ds(M + first(p), W)], out.at[0, pl.ds(first(p), W)]
        return remote(src, dst, fs.at[2, p], fr.at[2, p], other)

    def edge(src, dst, planes, slot, dev):
        near, beyond = (1 - flip) * (X - planes), M - planes + flip * (X + planes)
        return remote(src.at[pl.ds(near, planes)], dst.at[pl.ds(beyond, planes)], fs.at[3, slot], fr.at[3, slot], dev)

    base_edge = edge(fields.at[0], state.at[0], 2 * ITERS - 1, 0, mate)
    base_edge_across = edge(fields.at[0], state.at[0], 2 * ITERS - 1, 1, across)
    force_edge = edge(forcing, force, 2 * ITERS - 2, 2, mate)
    adjoint_edge = edge(fields.at[0], state.at[ITERS], ITERS, 3, mate)
    adjoint_edge_across = edge(fields.at[0], state.at[ITERS], ITERS, 4, across)

    def send_x(k, p):
        pl.when(jnp.logical_and(p == 0, has_far))(lambda: x_far(k).start())

    def recv_x(k, p):
        pl.when(jnp.logical_and(p == 0, has_far))(lambda: x_far(k).wait_recv())

    def send_y(k, p):
        pl.when(has_down)(lambda: y_down(k, p).start())
        pl.when(has_up)(lambda: y_up(k, p).start())

    def recv_y(k, p):
        pl.when(has_up)(lambda: y_down(k, p).wait_recv())
        pl.when(has_down)(lambda: y_up(k, p).wait_recv())

    force_in = pltpu.make_async_copy(forcing, force.at[pl.ds(M, X)], local.at[0])

    def own(k):
        return pltpu.make_async_copy(fields.at[0], state.at[k, pl.ds(M, X)], local.at[1])

    barrier = pltpu.get_barrier_semaphore()

    def greet(dev):
        pl.semaphore_signal(barrier, inc=1, device_id=dev, device_id_type=MESH)

    greet(other)
    greet(mate)
    pl.when(is_full)(lambda: greet(across))
    pl.when(has_far)(lambda: greet(far))
    pl.when(has_down)(lambda: greet(down))
    pl.when(has_up)(lambda: greet(up))
    pl.when(base_side)(lambda: own(0).start())
    pl.when(home_full)(lambda: own(ITERS).start())
    pl.when(works)(lambda: force_in.start())
    peers = 2 + full + has_far.astype(jnp.int32) + has_down.astype(jnp.int32) + has_up.astype(jnp.int32)
    pl.semaphore_wait(barrier, peers)

    @pl.when(base_only)
    def _():
        brick(0).start()
        base_edge.start()
        force_edge.start()

        @pl.loop(1, n)
        def _(p):
            brick(p).start()

    @pl.when(away_full)
    def _():
        base_edge_across.start()
        base_edge.start()
        force_edge.start()

    @pl.when(idle)
    def _():
        lent(0).start()
        adjoint_edge.start()
        force_edge.start()

        @pl.loop(1, n)
        def _(p):
            lent(p).start()

    @pl.when(home_full)
    def _():
        adjoint_edge_across.start()

    row = lax.broadcasted_iota(jnp.int32, (Y, Z), 0)
    lane = lax.broadcasted_iota(jnp.int32, (Y, Z), 1)

    def edge_rows(k, i, value):
        sy[k, 0, pl.ds(W + i, 1), :] = value[0:1]
        sy[k, 1, pl.ds(W + i, 1), :] = value[Y - 1 : Y]

    def edges_of(k, p):
        for j in range(W):
            i = first(p) + j
            sy[k, 0, pl.ds(W + i, 1), :] = state[k, M + i, 0:1]
            sy[k, 1, pl.ds(W + i, 1), :] = state[k, M + i, Y - 1 : Y]

    def around(k, i, mid):
        below = jnp.where(row == 0, yh[k, 0, pl.ds(W + i, 1), :], pltpu.roll(mid, 1, 0))
        above = jnp.where(row == Y - 1, yh[k, 1, pl.ds(W + i, 1), :], pltpu.roll(mid, Y - 1, 0))
        before = jnp.where(lane == 0, 0.0, pltpu.roll(mid, 1, 1))
        after = jnp.where(lane == Z - 1, 0.0, pltpu.roll(mid, Z - 1, 1))
        return (below + above) + (before + after)

    def forward(k, p, put):
        scale = level[k, 0:1, :]
        for j in range(W):
            i = first(p) + j
            mid, prev, nxt = state[k, M + i], state[k, M + i - 1], state[k, M + i + 1]
            total = around(k, i, mid) + (nxt + prev) - mid * (nxt - prev)
            put(i, 0.4 * mid + 0.1 * total + force[M + i] * scale)

    def backward(k, b, p, put):
        for j in range(W):
            i = first(p) + j
            mid, prev, nxt = state[k, M + i], state[k, M + i - 1], state[k, M + i + 1]
            total = around(k, i, mid) + (nxt + prev)
            total = total + state[b, M + i + 1] * (nxt - mid) - state[b, M + i - 1] * (prev - mid)
            put(i, 0.4 * mid + 0.1 * total)

    def into_level(k):
        def put(i, value):
            state[k, M + i] = value
            edge_rows(k, i, value)

        return put

    def into_return(i, value):
        state[2 * ITERS, M + i] = value

    def into_out(i, value):
        out[0, i] = value

    @pl.when(works)
    def _():
        for k in range(ITERS):
            phase = (step_ref[0] + k).astype(jnp.float32) * (2.0 * math.pi / 64.0)
            level[k] = 0.2 * jnp.sin(jnp.full((8, Z), phase, jnp.float32))

        @pl.loop(0, 2 * ITERS)
        def _(k):
            @pl.when(jnp.logical_not(has_far))
            def _():
                state[k, M - 1 + flip * (X + 1)] = jnp.zeros((Y, Z), jnp.float32)

            @pl.when(jnp.logical_not(has_down))
            def _():
                yh[k, 0] = jnp.zeros((X + 2 * W, Z), jnp.float32)

            @pl.when(jnp.logical_not(has_up))
            def _():
                yh[k, 1] = jnp.zeros((X + 2 * W, Z), jnp.float32)

        pl.when(base_side)(lambda: own(0).wait())
        pl.when(home_full)(lambda: own(ITERS).wait())
        force_in.wait()

        def begin(p):
            pl.when(jnp.logical_and(home_full, p < n))(lambda: brick(p).wait_recv())

            @pl.when(p == n)
            def _():
                pl.when(home_full)(lambda: base_edge_across.wait_recv())
                pl.when(base_side)(lambda: base_edge.wait_recv())
                force_edge.wait_recv()

            edges_of(0, p)
            send_x(0, p)
            send_y(0, p)

        def borrow(p):
            pl.when(jnp.logical_and(away_full, p < n))(lambda: lent(p).wait_recv())

            @pl.when(p == n)
            def _():
                pl.when(home_full)(lambda: adjoint_edge.wait_recv())
                pl.when(away_full)(lambda: adjoint_edge_across.wait_recv())

            edges_of(ITERS, p)
            send_x(ITERS, p)
            send_y(ITERS, p)

        def step_base(k, p):
            recv_x(k, p)
            recv_y(k, p)
            forward(k, p, into_level(k + 1))
            send_x(k + 1, p)
            pl.when(jnp.logical_or(k < ITERS - 2, jnp.logical_and(base_side, p < n)))(
                lambda: send_y(k + 1, p)
            )

        def last_base(p):
            pl.when(base_only)(lambda: recv_x(ITERS - 1, p))
            recv_y(ITERS - 1, p)
            forward(ITERS - 1, p, into_out)

        def step_adjoint(m, p):
            k, b = ITERS + m, ITERS - 1 - m
            pl.when(m == 0)(lambda: recv_x(ITERS - 1, p))
            recv_x(k, p)
            recv_y(k, p)
            backward(k, b, p, into_level(k + 1))
            send_x(k + 1, p)
            pl.when(jnp.logical_or(m < ITERS - 2, p < n))(lambda: send_y(k + 1, p))

        def last_adjoint(p):
            k, b = 2 * ITERS - 1, 0
            recv_x(k, p)
            recv_y(k, p)
            pl.when(home_full)(lambda: backward(k, b, p, into_out))
            pl.when(away_full)(lambda: backward(k, b, p, into_return))

        def task(p, hi, run, extra=None):
            ok = jnp.logical_and(p >= 0, p < hi)
            pl.when(ok if extra is None else jnp.logical_and(ok, extra))(functools.partial(run, p))

        @pl.loop(0, n + 2 * ITERS - 1)
        def _(t):
            task(t, n + 1, begin)

            @pl.loop(0, ITERS - 1)
            def _(k):
                task(t - 1 - k, n + 1, functools.partial(step_base, k))

            task(t - ITERS + 1, n + 1, borrow, is_full)

            @pl.loop(0, ITERS - 1)
            def _(m):
                task(t - ITERS - m, n + 1, functools.partial(step_adjoint, m), is_full)

            task(t - 2 * ITERS + 1, n, last_adjoint, is_full)

            @pl.when(jnp.logical_and(base_only, t == n - 1))
            def _():
                @pl.loop(0, n - 1)
                def _(p):
                    brick(p).wait_send()

                pl.semaphore_signal(go, inc=1, device_id=mate, device_id_type=MESH)

            @pl.when(jnp.logical_and(away_full, t == hold))
            def _():
                pl.semaphore_wait(go, 1)

                @pl.loop(0, hold - 2 * ITERS + 2)
                def _(p):
                    returned(p).start()

            @pl.when(jnp.logical_and(away_full, t > hold))
            def _():
                returned(t - 2 * ITERS + 1).start()

            task(t - ITERS, n, last_base, base_side)

        def sent_y(k, hi):
            @pl.loop(0, hi)
            def _(p):
                pl.when(has_down)(lambda: y_down(k, p).wait_send())
                pl.when(has_up)(lambda: y_up(k, p).wait_send())

        @pl.loop(0, ITERS - 1)
        def _(k):
            pl.when(has_far)(lambda: x_far(k).wait_send())
            sent_y(k, n + 1)

        pl.when(has_far)(lambda: x_far(ITERS - 1).wait_send())
        pl.when(base_side)(lambda: sent_y(ITERS - 1, n))

        @pl.when(is_full)
        def _():
            @pl.loop(ITERS, 2 * ITERS - 1)
            def _(k):
                pl.when(has_far)(lambda: x_far(k).wait_send())
                sent_y(k, n + 1)

            pl.when(has_far)(lambda: x_far(2 * ITERS - 1).wait_send())
            sent_y(2 * ITERS - 1, n)

    @pl.when(base_only)
    def _():
        brick(n - 1).wait_send()
        base_edge.wait_send()
        force_edge.wait_send()

    @pl.when(away_full)
    def _():
        base_edge_across.wait_send()
        base_edge.wait_send()
        force_edge.wait_send()

        @pl.loop(0, n)
        def _(p):
            returned(p).wait_send()

    @pl.when(home_full)
    def _():
        adjoint_edge_across.wait_send()

    @pl.when(idle)
    def _():

        @pl.loop(0, n)
        def _(p):
            lent(p).wait_send()

        adjoint_edge.wait_send()
        force_edge.wait_send()

        @pl.loop(0, n)
        def _(p):
            returned(p).wait_recv()


def on_device(fields, forcing, step_index):
    X, Y, Z = forcing.shape
    W = 8
    n = X // W
    assert X % W == 0 and lax.axis_size("gx") % 2 == 0 and W >= 2 * ITERS - 1
    levels = 2 * ITERS
    planes = X + 2 * W + 2
    return pl.pallas_call(
        functools.partial(window, W),
        out_shape=pltpu.VMEM(fields.shape, jnp.float32),
        in_specs=[pl.BlockSpec(memory_space=pltpu.SMEM)] + [pl.BlockSpec(memory_space=pltpu.HBM)] * 2,
        out_specs=pl.BlockSpec(memory_space=pltpu.VMEM),
        scratch_shapes=[
            pltpu.VMEM((levels + 1, planes, Y, Z), jnp.float32),
            pltpu.VMEM((levels, 2, X + 2 * W, Z), jnp.float32),
            pltpu.VMEM((levels, 2, X + 2 * W, Z), jnp.float32),
            pltpu.VMEM((planes, Y, Z), jnp.float32),
            pltpu.VMEM((ITERS, 8, Z), jnp.float32),
            pltpu.SemaphoreType.DMA((levels,)),
            pltpu.SemaphoreType.DMA((levels,)),
            pltpu.SemaphoreType.DMA((levels, 2, n + 1)),
            pltpu.SemaphoreType.DMA((levels, 2, n + 1)),
            pltpu.SemaphoreType.DMA((4, max(n, 5))),
            pltpu.SemaphoreType.DMA((4, max(n, 5))),
            pltpu.SemaphoreType.DMA((2,)),
            pltpu.SemaphoreType.REGULAR,
        ],
        compiler_params=pltpu.CompilerParams(
            collective_id=0, has_side_effects=True, vmem_limit_bytes=48 * 1024 * 1024
        ),
        name="window",
    )(step_index, *(pltpu.with_memory_space_constraint(a, pltpu.HBM) for a in (fields, forcing)))


def solution(mesh):
    placed = (P("half", "gx", "yz", None), P("gx", "yz", None), P())
    return jax.shard_map(
        on_device,
        mesh=mesh,
        in_specs=placed,
        out_specs=P("half", "gx", "yz", None),
        check_vma=False,
    )
```

```python
import functools
import math

import jax
import jax.numpy as jnp
from jax import lax
from jax.experimental import pallas as pl
from jax.experimental.pallas import tpu as pltpu
from jax.sharding import PartitionSpec as P

ITERS = 4
EARLY = 2
MESH = pl.DeviceIdType.MESH


def window(W, H, step_ref, fields, forcing, out, state, force, level, xs, xr, ys, yr, fs, fr, local, go):
    X, Y, Z = forcing.shape
    n = X // W
    M = W + 1
    R = Y + 2 * H
    rows = pl.ds(H, Y)
    hold = n + 1
    side = lax.axis_index("half")
    gx, nx = lax.axis_index("gx"), lax.axis_size("gx")
    gy, ny = lax.axis_index("yz"), lax.axis_size("yz")

    flip = lax.rem(gx, 2)
    home = lax.rem(lax.div(gx + 1, 2), 2)
    full = jnp.where(side == 1, home, 1 - home)
    base_side = side == 0
    is_full, is_home = full == 1, home == 1
    works = jnp.logical_or(base_side, is_full)
    away_full = jnp.logical_and(base_side, is_full)
    home_full = jnp.logical_and(side == 1, is_full)
    base_only = jnp.logical_and(base_side, is_home)
    idle = jnp.logical_and(side == 1, home == 0)

    has_far = jnp.logical_or(jnp.logical_and(flip == 0, gx > 0), jnp.logical_and(flip == 1, gx < nx - 1))
    has_down, has_up = gy > 0, gy < ny - 1
    far = {"gx": lax.rem(gx + nx - 1 + 2 * flip, nx)}
    mate = {"gx": gx + 1 - 2 * flip}
    down, up = {"yz": lax.rem(gy + ny - 1, ny)}, {"yz": lax.rem(gy + 1, ny)}
    other = {"half": 1 - side}
    across = {"half": 1 - side, "gx": gx + 1 - 2 * flip}

    def first(p):
        return p * W + flip * (X - (2 * p + 1) * W)

    def remote(src, dst, s, r, dev):
        return pltpu.make_async_remote_copy(
            src_ref=src, dst_ref=dst, send_sem=s, recv_sem=r, device_id=dev, device_id_type=MESH
        )

    def x_far(k):
        src, dst = M + flip * (X - 1), M + X - flip * (X + 1)
        return remote(state.at[k, src], state.at[k, dst], xs.at[k], xr.at[k], far)

    sources = (state.at[0], state.at[ITERS], force)

    def y_down(k, p):
        src = sources[k].at[pl.ds(M + first(p), W)]
        return remote(src.at[:, pl.ds(H, H)], src.at[:, pl.ds(H + Y, H)], ys.at[k, 0, p], yr.at[k, 0, p], down)

    def y_up(k, p):
        src = sources[k].at[pl.ds(M + first(p), W)]
        return remote(src.at[:, pl.ds(Y, H)], src.at[:, pl.ds(0, H)], ys.at[k, 1, p], yr.at[k, 1, p], up)

    def brick(p):
        src, dst = fields.at[0, pl.ds(first(p), W)], state.at[0, pl.ds(M + first(p), W), rows]
        return remote(src, dst, fs.at[0, p], fr.at[0, p], other)

    def lent(p):
        src, dst = fields.at[0, pl.ds(first(p), W)], state.at[ITERS, pl.ds(M + first(p), W), rows]
        return remote(src, dst, fs.at[1, p], fr.at[1, p], other)

    def returned(p):
        src, dst = state.at[2 * ITERS, pl.ds(M + first(p), W), rows], out.at[0, pl.ds(first(p), W)]
        return remote(src, dst, fs.at[2, p], fr.at[2, p], other)

    def edge(src, dst, planes, slot, dev):
        near, beyond = (1 - flip) * (X - planes), M - planes + flip * (X + planes)
        src, dst = src.at[pl.ds(near, planes)], dst.at[pl.ds(beyond, planes), rows]
        return remote(src, dst, fs.at[3, slot], fr.at[3, slot], dev)

    base_edge = edge(fields.at[0], state.at[0], 2 * ITERS - 1, 0, mate)
    base_edge_across = edge(fields.at[0], state.at[0], 2 * ITERS - 1, 1, across)
    force_edge = edge(forcing, force, 2 * ITERS - 2, 2, mate)
    adjoint_edge = edge(fields.at[0], state.at[ITERS], ITERS, 3, mate)
    adjoint_edge_across = edge(fields.at[0], state.at[ITERS], ITERS, 4, across)

    def send_x(k, p):
        pl.when(jnp.logical_and(p == 0, has_far))(lambda: x_far(k).start())

    def recv_x(k, p):
        pl.when(jnp.logical_and(p == 0, has_far))(lambda: x_far(k).wait_recv())

    def send_y(k, p):
        pl.when(has_down)(lambda: y_down(k, p).start())
        pl.when(has_up)(lambda: y_up(k, p).start())

    def recv_y(k, p):
        pl.when(has_up)(lambda: y_down(k, p).wait_recv())
        pl.when(has_down)(lambda: y_up(k, p).wait_recv())

    force_in = pltpu.make_async_copy(forcing, force.at[pl.ds(M, X), rows], local.at[0])

    def own(k):
        return pltpu.make_async_copy(fields.at[0], state.at[k, pl.ds(M, X), rows], local.at[1])

    barrier = pltpu.get_barrier_semaphore()

    def greet(dev):
        pl.semaphore_signal(barrier, inc=1, device_id=dev, device_id_type=MESH)

    greet(other)
    greet(mate)
    pl.when(is_full)(lambda: greet(across))
    pl.when(has_far)(lambda: greet(far))
    pl.when(has_down)(lambda: greet(down))
    pl.when(has_up)(lambda: greet(up))
    pl.when(base_side)(lambda: own(0).start())
    pl.when(home_full)(lambda: own(ITERS).start())
    pl.when(works)(lambda: force_in.start())
    peers = 2 + full + has_far.astype(jnp.int32) + has_down.astype(jnp.int32) + has_up.astype(jnp.int32)
    pl.semaphore_wait(barrier, peers)

    @pl.when(base_only)
    def _():
        brick(0).start()
        base_edge.start()
        force_edge.start()

        @pl.loop(1, n)
        def _(p):
            brick(p).start()

    @pl.when(away_full)
    def _():
        base_edge_across.start()
        base_edge.start()
        force_edge.start()

    @pl.when(idle)
    def _():
        lent(0).start()
        adjoint_edge.start()
        force_edge.start()

        @pl.loop(1, n)
        def _(p):
            lent(p).start()

    @pl.when(home_full)
    def _():
        adjoint_edge_across.start()

    lane = lax.broadcasted_iota(jnp.int32, (R, Z), 1)
    low = jnp.broadcast_to(has_down, (H, Z))
    high = jnp.broadcast_to(has_up, (H, Z))

    def around(mid):
        below, above = pltpu.roll(mid, 1, 0), pltpu.roll(mid, R - 1, 0)
        before = jnp.where(lane == 0, 0.0, pltpu.roll(mid, 1, 1))
        after = jnp.where(lane == Z - 1, 0.0, pltpu.roll(mid, Z - 1, 1))
        return (below + above) + (before + after)

    def forward(k, p, put):
        scale = level[k, 0:1, :]
        for j in range(W):
            i = first(p) + j
            mid, prev, nxt = state[k, M + i], state[k, M + i - 1], state[k, M + i + 1]
            total = around(mid) + (nxt + prev) - mid * (nxt - prev)
            put(i, 0.4 * mid + 0.1 * total + force[M + i] * scale)

    def backward(k, b, p, put):
        for j in range(W):
            i = first(p) + j
            mid, prev, nxt = state[k, M + i], state[k, M + i - 1], state[k, M + i + 1]
            total = around(mid) + (nxt + prev)
            total = total + state[b, M + i + 1] * (nxt - mid) - state[b, M + i - 1] * (prev - mid)
            put(i, 0.4 * mid + 0.1 * total)

    def into_level(k):
        def put(i, value):
            state[k, M + i, 0:H] = jnp.where(low, value[0:H], 0.0)
            state[k, M + i, H : H + Y] = value[H : H + Y]
            state[k, M + i, H + Y : R] = jnp.where(high, value[H + Y : R], 0.0)

        return put

    def into_return(i, value):
        state[2 * ITERS, M + i, H : H + Y] = value[H : H + Y]

    def into_out(i, value):
        out[0, i] = value[H : H + Y]

    @pl.when(works)
    def _():
        for k in range(ITERS):
            phase = (step_ref[0] + k).astype(jnp.float32) * (2.0 * math.pi / 64.0)
            level[k] = 0.2 * jnp.sin(jnp.full((8, Z), phase, jnp.float32))

        @pl.loop(0, 2 * ITERS)
        def _(k):
            @pl.when(jnp.logical_not(has_far))
            def _():
                state[k, M - 1 + flip * (X + 1)] = jnp.zeros((R, Z), jnp.float32)

        def clear(at):
            @pl.loop(0, X + W)
            def _(i):
                state[0, M - flip * W + i, at] = jnp.zeros((H, Z), jnp.float32)
                state[ITERS, M - flip * W + i, at] = jnp.zeros((H, Z), jnp.float32)

        pl.when(jnp.logical_not(has_down))(lambda: clear(pl.ds(0, H)))
        pl.when(jnp.logical_not(has_up))(lambda: clear(pl.ds(H + Y, H)))
        pl.when(base_side)(lambda: own(0).wait())
        pl.when(home_full)(lambda: own(ITERS).wait())
        force_in.wait()

        @pl.loop(0, n)
        def _(p):
            pl.when(base_side)(lambda: send_y(0, p))
            send_y(2, p)
            pl.when(home_full)(lambda: send_y(1, p))

        def begin(p):
            pl.when(jnp.logical_and(home_full, p < n))(lambda: brick(p).wait_recv())

            @pl.when(p == n)
            def _():
                pl.when(home_full)(lambda: base_edge_across.wait_recv())
                pl.when(base_side)(lambda: base_edge.wait_recv())
                force_edge.wait_recv()

            pl.when(jnp.logical_or(home_full, p == n))(lambda: send_y(0, p))
            pl.when(p == n)(lambda: send_y(2, p))

        def gather(p):
            recv_y(0, p)
            recv_y(2, p)
            send_x(0, p)

        def borrow(p):
            pl.when(jnp.logical_and(away_full, p < n))(lambda: lent(p).wait_recv())

            @pl.when(p == n)
            def _():
                pl.when(home_full)(lambda: adjoint_edge.wait_recv())
                pl.when(away_full)(lambda: adjoint_edge_across.wait_recv())

            pl.when(jnp.logical_or(away_full, p == n))(lambda: send_y(1, p))

        def gather_adjoint(p):
            recv_y(1, p)
            send_x(ITERS, p)

        def step_base(k, p):
            recv_x(k, p)
            forward(k, p, into_level(k + 1))
            send_x(k + 1, p)

        def last_base(p):
            pl.when(base_only)(lambda: recv_x(ITERS - 1, p))
            forward(ITERS - 1, p, into_out)

        def step_adjoint(m, p):
            k, b = ITERS + m, ITERS - 1 - m
            pl.when(m == 0)(lambda: recv_x(ITERS - 1, p))
            recv_x(k, p)
            backward(k, b, p, into_level(k + 1))
            send_x(k + 1, p)

        def last_adjoint(p):
            k, b = 2 * ITERS - 1, 0
            recv_x(k, p)
            pl.when(home_full)(lambda: backward(k, b, p, into_out))
            pl.when(away_full)(lambda: backward(k, b, p, into_return))

        def task(p, hi, run, extra=None):
            ok = jnp.logical_and(p >= 0, p < hi)
            pl.when(ok if extra is None else jnp.logical_and(ok, extra))(functools.partial(run, p))

        @pl.loop(0, n + 2 * ITERS + 1)
        def _(t):
            task(t, n + 1, begin)
            task(t - 2, n + 1, gather)

            @pl.loop(0, ITERS - 1)
            def _(k):
                task(t - 3 - k, n + 1, functools.partial(step_base, k))

            task(t - ITERS + 1, n + 1, borrow, is_full)
            task(t - ITERS - 1, n + 1, gather_adjoint, is_full)

            @pl.loop(0, ITERS - 1)
            def _(m):
                task(t - ITERS - 2 - m, n + 1, functools.partial(step_adjoint, m), is_full)

            task(t - 2 * ITERS - 1, n, last_adjoint, is_full)

            @pl.when(jnp.logical_and(away_full, t == hold))
            def _():
                pl.semaphore_wait(go, 1)

                @pl.loop(0, hold - 2 * ITERS)
                def _(p):
                    returned(p).start()

            @pl.when(jnp.logical_and(away_full, t > hold))
            def _():
                returned(t - 2 * ITERS - 1).start()

            task(t - ITERS - 2, n, last_base, base_side)

            @pl.when(jnp.logical_and(base_only, t == 7))
            def _():
                @pl.loop(0, n - EARLY)
                def _(p):
                    brick(p).wait_send()

                pl.semaphore_signal(go, inc=1, device_id=mate, device_id_type=MESH)

        def sent_y(k):
            @pl.loop(0, n + 1)
            def _(p):
                pl.when(has_down)(lambda: y_down(k, p).wait_send())
                pl.when(has_up)(lambda: y_up(k, p).wait_send())

        def sent_x(lo, hi):
            @pl.loop(lo, hi)
            def _(k):
                pl.when(has_far)(lambda: x_far(k).wait_send())

        sent_x(0, ITERS)
        sent_y(0)
        sent_y(2)

        @pl.when(is_full)
        def _():
            sent_x(ITERS, 2 * ITERS)
            sent_y(1)

    @pl.when(base_only)
    def _():
        @pl.loop(n - EARLY, n)
        def _(p):
            brick(p).wait_send()

        base_edge.wait_send()
        force_edge.wait_send()

    @pl.when(away_full)
    def _():
        base_edge_across.wait_send()
        base_edge.wait_send()
        force_edge.wait_send()

        @pl.loop(0, n)
        def _(p):
            returned(p).wait_send()

    @pl.when(home_full)
    def _():
        adjoint_edge_across.wait_send()

    @pl.when(idle)
    def _():

        @pl.loop(0, n)
        def _(p):
            lent(p).wait_send()

        adjoint_edge.wait_send()
        force_edge.wait_send()

        @pl.loop(0, n)
        def _(p):
            returned(p).wait_recv()


def on_device(fields, forcing, step_index):
    X, Y, Z = forcing.shape
    W = H = 8
    n = X // W
    assert X % W == 0 and lax.axis_size("gx") % 2 == 0 and W >= 2 * ITERS - 1 and Y >= 2 * H
    levels = 2 * ITERS
    planes = X + 2 * W + 2
    return pl.pallas_call(
        functools.partial(window, W, H),
        out_shape=pltpu.VMEM(fields.shape, jnp.float32),
        in_specs=[pl.BlockSpec(memory_space=pltpu.SMEM)] + [pl.BlockSpec(memory_space=pltpu.HBM)] * 2,
        out_specs=pl.BlockSpec(memory_space=pltpu.VMEM),
        scratch_shapes=[
            pltpu.VMEM((levels + 1, planes, Y + 2 * H, Z), jnp.float32),
            pltpu.VMEM((planes, Y + 2 * H, Z), jnp.float32),
            pltpu.VMEM((ITERS, 8, Z), jnp.float32),
            pltpu.SemaphoreType.DMA((levels,)),
            pltpu.SemaphoreType.DMA((levels,)),
            pltpu.SemaphoreType.DMA((3, 2, n + 1)),
            pltpu.SemaphoreType.DMA((3, 2, n + 1)),
            pltpu.SemaphoreType.DMA((4, max(n, 5))),
            pltpu.SemaphoreType.DMA((4, max(n, 5))),
            pltpu.SemaphoreType.DMA((2,)),
            pltpu.SemaphoreType.REGULAR,
        ],
        compiler_params=pltpu.CompilerParams(
            collective_id=0, has_side_effects=True, vmem_limit_bytes=48 * 1024 * 1024
        ),
        name="window",
    )(step_index, *(pltpu.with_memory_space_constraint(a, pltpu.HBM) for a in (fields, forcing)))


def solution(mesh):
    placed = (P("half", "gx", "yz", None), P("gx", "yz", None), P())
    return jax.shard_map(
        on_device,
        mesh=mesh,
        in_specs=placed,
        out_specs=P("half", "gx", "yz", None),
        check_vma=False,
    )
```

```python
import functools
import math

import jax
import jax.numpy as jnp
from jax import lax
from jax.experimental import pallas as pl
from jax.experimental.pallas import tpu as pltpu
from jax.sharding import PartitionSpec as P

ITERS = 4
EARLY = 3
AHEAD = 2
MESH = pl.DeviceIdType.MESH


def window(W, H, step_ref, fields, forcing, out, state, force, level, ys, yr, fs, fr, local, go):
    X, Y, Z = forcing.shape
    n = X // W
    M = W + 1
    R = Y + 2 * H
    rows = pl.ds(H, Y)
    hold = n + 1
    side = lax.axis_index("half")
    gx, nx = lax.axis_index("gx"), lax.axis_size("gx")
    gy, ny = lax.axis_index("yz"), lax.axis_size("yz")

    flip = lax.rem(gx, 2)
    home = lax.rem(lax.div(gx + 1, 2), 2)
    full = jnp.where(side == 1, home, 1 - home)
    base_side = side == 0
    is_full, is_home = full == 1, home == 1
    works = jnp.logical_or(base_side, is_full)
    away_full = jnp.logical_and(base_side, is_full)
    home_full = jnp.logical_and(side == 1, is_full)
    base_only = jnp.logical_and(base_side, is_home)
    idle = jnp.logical_and(side == 1, home == 0)

    has_far = jnp.logical_or(jnp.logical_and(flip == 0, gx > 0), jnp.logical_and(flip == 1, gx < nx - 1))
    has_down, has_up = gy > 0, gy < ny - 1
    far = {"gx": lax.rem(gx + nx - 1 + 2 * flip, nx)}
    mate = {"gx": gx + 1 - 2 * flip}
    down, up = {"yz": lax.rem(gy + ny - 1, ny)}, {"yz": lax.rem(gy + 1, ny)}
    other = {"half": 1 - side}
    across = {"half": 1 - side, "gx": gx + 1 - 2 * flip}

    def first(p):
        return p * W + flip * (X - (2 * p + 1) * W)

    def remote(src, dst, s, r, dev):
        return pltpu.make_async_remote_copy(
            src_ref=src, dst_ref=dst, send_sem=s, recv_sem=r, device_id=dev, device_id_type=MESH
        )

    sources = (state.at[0], state.at[ITERS], force)

    def y_down(k, p):
        src = sources[k].at[pl.ds(M + first(p), W)]
        return remote(src.at[:, pl.ds(H, H)], src.at[:, pl.ds(H + Y, H)], ys.at[k, 0, p + 1], yr.at[k, 0, p + 1], down)

    def y_up(k, p):
        src = sources[k].at[pl.ds(M + first(p), W)]
        return remote(src.at[:, pl.ds(Y, H)], src.at[:, pl.ds(0, H)], ys.at[k, 1, p + 1], yr.at[k, 1, p + 1], up)

    def brick(p):
        src, dst = fields.at[0, pl.ds(first(p), W)], state.at[0, pl.ds(M + first(p), W), rows]
        return remote(src, dst, fs.at[0, p], fr.at[0, p], other)

    def lent(p):
        src, dst = fields.at[0, pl.ds(first(p), W)], state.at[ITERS, pl.ds(M + first(p), W), rows]
        return remote(src, dst, fs.at[1, p], fr.at[1, p], other)

    def returned(p):
        src, dst = state.at[2 * ITERS, pl.ds(M + first(p), W), rows], out.at[0, pl.ds(first(p), W)]
        return remote(src, dst, fs.at[2, p], fr.at[2, p], other)

    def edge(src, dst, planes, slot, dev):
        near, beyond = (1 - flip) * (X - planes), M - planes + flip * (X + planes)
        src, dst = src.at[pl.ds(near, planes)], dst.at[pl.ds(beyond, planes), rows]
        return remote(src, dst, fs.at[3, slot], fr.at[3, slot], dev)

    base_edge = edge(fields.at[0], state.at[0], 2 * ITERS - 1, 0, mate)
    base_edge_across = edge(fields.at[0], state.at[0], 2 * ITERS - 1, 1, across)
    force_edge = edge(forcing, force, 2 * ITERS - 2, 2, mate)
    adjoint_edge = edge(fields.at[0], state.at[ITERS], ITERS, 3, mate)
    adjoint_edge_across = edge(fields.at[0], state.at[ITERS], ITERS, 4, across)

    def far_edge(src, dst, planes, slot):
        near, beyond = flip * (X - planes), M + X - flip * (X + planes)
        src, dst = src.at[pl.ds(near, planes)], dst.at[pl.ds(beyond, planes), rows]
        return remote(src, dst, fs.at[3, slot], fr.at[3, slot], far)

    own_base = state.at[0, pl.ds(M, X), rows]
    own_adjoint = state.at[ITERS, pl.ds(M, X), rows]
    base_far = far_edge(fields.at[0], state.at[0], 2 * ITERS - 1, 5)
    base_far_on = far_edge(own_base, state.at[0], 2 * ITERS - 1, 5)
    force_far = far_edge(forcing, force, 2 * ITERS - 2, 6)
    adjoint_far = far_edge(fields.at[0], state.at[ITERS], ITERS, 7)
    adjoint_far_on = far_edge(own_adjoint, state.at[ITERS], ITERS, 7)

    def send_y(k, p):
        pl.when(has_down)(lambda: y_down(k, p).start())
        pl.when(has_up)(lambda: y_up(k, p).start())

    def recv_y(k, p):
        pl.when(has_up)(lambda: y_down(k, p).wait_recv())
        pl.when(has_down)(lambda: y_up(k, p).wait_recv())

    force_in = pltpu.make_async_copy(forcing, force.at[pl.ds(M, X), rows], local.at[0])

    def own(k):
        return pltpu.make_async_copy(fields.at[0], state.at[k, pl.ds(M, X), rows], local.at[1])

    barrier = pltpu.get_barrier_semaphore()

    def greet(dev):
        pl.semaphore_signal(barrier, inc=1, device_id=dev, device_id_type=MESH)

    greet(other)
    greet(mate)
    pl.when(is_full)(lambda: greet(across))
    pl.when(has_far)(lambda: greet(far))
    pl.when(has_down)(lambda: greet(down))
    pl.when(has_up)(lambda: greet(up))
    pl.when(base_side)(lambda: own(0).start())
    pl.when(home_full)(lambda: own(ITERS).start())
    pl.when(works)(lambda: force_in.start())
    peers = 2 + full + has_far.astype(jnp.int32) + has_down.astype(jnp.int32) + has_up.astype(jnp.int32)
    pl.semaphore_wait(barrier, peers)

    @pl.when(base_only)
    def _():
        brick(0).start()
        base_edge.start()
        force_edge.start()

        @pl.when(has_far)
        def _():
            base_far.start()
            force_far.start()

        @pl.loop(1, n)
        def _(p):
            brick(p).start()

    @pl.when(away_full)
    def _():
        base_edge_across.start()

        @pl.when(has_far)
        def _():
            base_far.start()
            force_far.start()

        base_edge.start()
        force_edge.start()

    @pl.when(idle)
    def _():
        lent(0).start()
        adjoint_edge.start()
        force_edge.start()

        @pl.loop(1, n)
        def _(p):
            lent(p).start()

    @pl.when(home_full)
    def _():
        adjoint_edge_across.start()

        @pl.when(has_far)
        def _():
            adjoint_far.start()
            force_far.start()

    lane = lax.broadcasted_iota(jnp.int32, (R, Z), 1)
    low = jnp.broadcast_to(has_down, (H, Z))
    high = jnp.broadcast_to(has_up, (H, Z))

    def around(mid):
        below, above = pltpu.roll(mid, 1, 0), pltpu.roll(mid, R - 1, 0)
        before = jnp.where(lane == 0, 0.0, pltpu.roll(mid, 1, 1))
        after = jnp.where(lane == Z - 1, 0.0, pltpu.roll(mid, Z - 1, 1))
        return (below + above) + (before + after)

    def forward(k, p, put):
        scale = level[k, 0:1, :]
        for j in range(W):
            i = first(p) + j
            mid, prev, nxt = state[k, M + i], state[k, M + i - 1], state[k, M + i + 1]
            total = around(mid) + (nxt + prev) - mid * (nxt - prev)
            put(i, 0.4 * mid + 0.1 * total + force[M + i] * scale)

    def backward(k, b, p, put):
        for j in range(W):
            i = first(p) + j
            mid, prev, nxt = state[k, M + i], state[k, M + i - 1], state[k, M + i + 1]
            total = around(mid) + (nxt + prev)
            total = total + state[b, M + i + 1] * (nxt - mid) - state[b, M + i - 1] * (prev - mid)
            put(i, 0.4 * mid + 0.1 * total)

    def into_level(k):
        def put(i, value):
            state[k, M + i, 0:H] = jnp.where(low, value[0:H], 0.0)
            state[k, M + i, H : H + Y] = value[H : H + Y]
            state[k, M + i, H + Y : R] = jnp.where(high, value[H + Y : R], 0.0)

        return put

    def into_return(i, value):
        state[2 * ITERS, M + i, H : H + Y] = value[H : H + Y]

    def into_out(i, value):
        out[0, i] = value[H : H + Y]

    @pl.when(works)
    def _():
        for k in range(ITERS):
            phase = (step_ref[0] + k).astype(jnp.float32) * (2.0 * math.pi / 64.0)
            level[k] = 0.2 * jnp.sin(jnp.full((8, Z), phase, jnp.float32))

        @pl.loop(0, 2 * ITERS)
        def _(k):
            @pl.when(jnp.logical_not(has_far))
            def _():
                state[k, M - 1 + flip * (X + 1)] = jnp.zeros((R, Z), jnp.float32)

        def clear(at):
            @pl.loop(0, X + W)
            def _(i):
                state[0, M - flip * W + i, at] = jnp.zeros((H, Z), jnp.float32)
                state[ITERS, M - flip * W + i, at] = jnp.zeros((H, Z), jnp.float32)

        pl.when(jnp.logical_not(has_down))(lambda: clear(pl.ds(0, H)))
        pl.when(jnp.logical_not(has_up))(lambda: clear(pl.ds(H + Y, H)))
        pl.when(base_side)(lambda: own(0).wait())
        pl.when(home_full)(lambda: own(ITERS).wait())
        force_in.wait()

        def ahead(p):
            pl.when(base_side)(lambda: send_y(0, p))
            send_y(2, p)
            pl.when(home_full)(lambda: send_y(1, p))

        pl.loop(0, AHEAD)(ahead)

        def begin(p):
            pl.when(jnp.logical_and(home_full, p < n))(lambda: brick(p).wait_recv())
            pl.when(jnp.logical_and(jnp.logical_and(home_full, has_far), p == 0))(lambda: base_far_on.start())

            @pl.when(p == n)
            def _():
                pl.when(home_full)(lambda: base_edge_across.wait_recv())
                pl.when(base_side)(lambda: base_edge.wait_recv())
                force_edge.wait_recv()

            pl.when(jnp.logical_or(home_full, p == n))(lambda: send_y(0, p))
            pl.when(p == n)(lambda: send_y(2, p))

        def begin_far():
            base_far.wait_recv()
            force_far.wait_recv()
            send_y(0, -1)
            send_y(2, -1)

        def gather(p):
            recv_y(0, p)
            recv_y(2, p)

        def borrow(p):
            pl.when(jnp.logical_and(away_full, p < n))(lambda: lent(p).wait_recv())
            pl.when(jnp.logical_and(jnp.logical_and(away_full, has_far), p == 0))(lambda: adjoint_far_on.start())

            @pl.when(p == n)
            def _():
                pl.when(home_full)(lambda: adjoint_edge.wait_recv())
                pl.when(away_full)(lambda: adjoint_edge_across.wait_recv())

            pl.when(jnp.logical_or(away_full, p == n))(lambda: send_y(1, p))

        def borrow_far():
            adjoint_far.wait_recv()
            send_y(1, -1)

        def gather_adjoint(p):
            recv_y(1, p)

        def step_base(k, p):
            forward(k, p, into_level(k + 1))

        def last_base(p):
            forward(ITERS - 1, p, into_out)

        def step_adjoint(m, p):
            k, b = ITERS + m, ITERS - 1 - m
            backward(k, b, p, into_level(k + 1))

        def last_adjoint(p):
            k, b = 2 * ITERS - 1, 0
            pl.when(home_full)(lambda: backward(k, b, p, into_out))
            pl.when(away_full)(lambda: backward(k, b, p, into_return))

        lowest = -has_far.astype(jnp.int32)
        full_far = jnp.logical_and(is_full, has_far)

        def task(p, hi, run, extra=None, lo=0):
            ok = jnp.logical_and(p >= lo, p < hi)
            pl.when(ok if extra is None else jnp.logical_and(ok, extra))(functools.partial(run, p))

        @pl.loop(0, n + 2 * ITERS + 1)
        def _(t):
            pl.when(t + AHEAD < n)(lambda: ahead(t + AHEAD))
            task(t, n + 1, begin)
            pl.when(jnp.logical_and(has_far, t == 1))(begin_far)
            task(t - 2, n + 1, gather)
            pl.when(jnp.logical_and(has_far, t == 2))(lambda: gather(-1))

            @pl.loop(0, ITERS - 1)
            def _(k):
                task(t - 3 - k, n + 1, functools.partial(step_base, k), lo=lowest)

            task(t - ITERS, n + 1, borrow, is_full)
            pl.when(jnp.logical_and(full_far, t == ITERS))(borrow_far)
            task(t - ITERS - 1, n + 1, gather_adjoint, is_full)
            pl.when(jnp.logical_and(full_far, t == ITERS + 1))(lambda: gather_adjoint(-1))

            @pl.loop(0, ITERS - 1)
            def _(m):
                task(t - ITERS - 2 - m, n + 1, functools.partial(step_adjoint, m), is_full, lowest)

            task(t - 2 * ITERS - 1, n, last_adjoint, is_full)

            @pl.when(jnp.logical_and(away_full, t == hold))
            def _():
                pl.semaphore_wait(go, 1)

                @pl.loop(0, hold - 2 * ITERS)
                def _(p):
                    returned(p).start()

            @pl.when(jnp.logical_and(away_full, t > hold))
            def _():
                returned(t - 2 * ITERS - 1).start()

            task(t - ITERS - 2, n, last_base, base_side)

            @pl.when(jnp.logical_and(base_only, t == 7))
            def _():
                @pl.loop(0, n - EARLY)
                def _(p):
                    brick(p).wait_send()

                pl.semaphore_signal(go, inc=1, device_id=mate, device_id_type=MESH)

        def sent_y(k):
            @pl.loop(lowest, n + 1)
            def _(p):
                pl.when(has_down)(lambda: y_down(k, p).wait_send())
                pl.when(has_up)(lambda: y_up(k, p).wait_send())

        sent_y(0)
        sent_y(2)
        pl.when(is_full)(lambda: sent_y(1))

        @pl.when(has_far)
        def _():
            base_far.wait_send()
            force_far.wait_send()
            pl.when(is_full)(lambda: adjoint_far.wait_send())

    @pl.when(base_only)
    def _():
        @pl.loop(n - EARLY, n)
        def _(p):
            brick(p).wait_send()

        base_edge.wait_send()
        force_edge.wait_send()

    @pl.when(away_full)
    def _():
        base_edge_across.wait_send()
        base_edge.wait_send()
        force_edge.wait_send()

        @pl.loop(0, n)
        def _(p):
            returned(p).wait_send()

    @pl.when(home_full)
    def _():
        adjoint_edge_across.wait_send()

    @pl.when(idle)
    def _():

        @pl.loop(0, n)
        def _(p):
            lent(p).wait_send()

        adjoint_edge.wait_send()
        force_edge.wait_send()

        @pl.loop(0, n)
        def _(p):
            returned(p).wait_recv()


def on_device(fields, forcing, step_index):
    X, Y, Z = forcing.shape
    W = H = 8
    n = X // W
    assert X % W == 0 and lax.axis_size("gx") % 2 == 0 and W >= 2 * ITERS - 1 and Y >= 2 * H
    levels = 2 * ITERS
    planes = X + 2 * W + 2
    return pl.pallas_call(
        functools.partial(window, W, H),
        out_shape=pltpu.VMEM(fields.shape, jnp.float32),
        in_specs=[pl.BlockSpec(memory_space=pltpu.SMEM)] + [pl.BlockSpec(memory_space=pltpu.HBM)] * 2,
        out_specs=pl.BlockSpec(memory_space=pltpu.VMEM),
        scratch_shapes=[
            pltpu.VMEM((levels + 1, planes, Y + 2 * H, Z), jnp.float32),
            pltpu.VMEM((planes, Y + 2 * H, Z), jnp.float32),
            pltpu.VMEM((ITERS, 8, Z), jnp.float32),
            pltpu.SemaphoreType.DMA((3, 2, n + 2)),
            pltpu.SemaphoreType.DMA((3, 2, n + 2)),
            pltpu.SemaphoreType.DMA((4, max(n, 8))),
            pltpu.SemaphoreType.DMA((4, max(n, 8))),
            pltpu.SemaphoreType.DMA((2,)),
            pltpu.SemaphoreType.REGULAR,
        ],
        compiler_params=pltpu.CompilerParams(
            collective_id=0, has_side_effects=True, vmem_limit_bytes=48 * 1024 * 1024
        ),
        name="window",
    )(step_index, *(pltpu.with_memory_space_constraint(a, pltpu.HBM) for a in (fields, forcing)))


def solution(mesh):
    placed = (P("half", "gx", "yz", None), P("gx", "yz", None), P())
    return jax.shard_map(
        on_device,
        mesh=mesh,
        in_specs=placed,
        out_specs=P("half", "gx", "yz", None),
        check_vma=False,
    )
```

```python
import functools
import math

import jax
import jax.numpy as jnp
from jax import lax
from jax.experimental import pallas as pl
from jax.experimental.pallas import tpu as pltpu
from jax.sharding import PartitionSpec as P

ITERS = 4
EARLY = 3
AHEAD = 2
FROM = 3
MESH = pl.DeviceIdType.MESH


def window(W, H, step_ref, fields, forcing, out, state, force, level, ys, yr, fs, fr, local, go):
    X, Y, Z = forcing.shape
    n = X // W
    M = W + 1
    R = Y + 2 * H
    rows = pl.ds(H, Y)
    hold = n + 1
    side = lax.axis_index("half")
    gx, nx = lax.axis_index("gx"), lax.axis_size("gx")
    gy, ny = lax.axis_index("yz"), lax.axis_size("yz")

    flip = lax.rem(gx, 2)
    home = lax.rem(lax.div(gx + 1, 2), 2)
    full = jnp.where(side == 1, home, 1 - home)
    base_side = side == 0
    is_full, is_home = full == 1, home == 1
    works = jnp.logical_or(base_side, is_full)
    away_full = jnp.logical_and(base_side, is_full)
    home_full = jnp.logical_and(side == 1, is_full)
    base_only = jnp.logical_and(base_side, is_home)
    idle = jnp.logical_and(side == 1, home == 0)

    has_far = jnp.logical_or(jnp.logical_and(flip == 0, gx > 0), jnp.logical_and(flip == 1, gx < nx - 1))
    has_down, has_up = gy > 0, gy < ny - 1
    far = {"gx": lax.rem(gx + nx - 1 + 2 * flip, nx)}
    mate = {"gx": gx + 1 - 2 * flip}
    down, up = {"yz": lax.rem(gy + ny - 1, ny)}, {"yz": lax.rem(gy + 1, ny)}
    other = {"half": 1 - side}
    across = {"half": 1 - side, "gx": gx + 1 - 2 * flip}

    def first(p, flip=flip):
        return p * W + flip * (X - (2 * p + 1) * W)

    def shared(p):
        return jnp.logical_and(p >= FROM, lax.rem(p - FROM, 2) == 0)

    def remote(src, dst, s, r, dev):
        return pltpu.make_async_remote_copy(
            src_ref=src, dst_ref=dst, send_sem=s, recv_sem=r, device_id=dev, device_id_type=MESH
        )

    sources = (state.at[0], state.at[ITERS], force)

    def y_down(k, p):
        src = sources[k].at[pl.ds(M + first(p), W)]
        return remote(src.at[:, pl.ds(H, H)], src.at[:, pl.ds(H + Y, H)], ys.at[k, 0, p + 1], yr.at[k, 0, p + 1], down)

    def y_up(k, p):
        src = sources[k].at[pl.ds(M + first(p), W)]
        return remote(src.at[:, pl.ds(Y, H)], src.at[:, pl.ds(0, H)], ys.at[k, 1, p + 1], yr.at[k, 1, p + 1], up)

    def brick(p):
        src, dst = fields.at[0, pl.ds(first(p), W)], state.at[0, pl.ds(M + first(p), W), rows]
        return remote(src, dst, fs.at[0, p], fr.at[0, p], other)

    def lent(p):
        src, dst = fields.at[0, pl.ds(first(p), W)], state.at[ITERS, pl.ds(M + first(p), W), rows]
        return remote(src, dst, fs.at[1, p], fr.at[1, p], other)

    def returned(p):
        src, dst = state.at[2 * ITERS, pl.ds(M + first(p), W), rows], out.at[0, pl.ds(first(p), W)]
        return remote(src, dst, fs.at[2, p], fr.at[2, p], other)

    def pass_on(p, flip):
        part = state.at[2 * ITERS, pl.ds(M + first(p, flip), W), rows]
        return remote(part, part, fs.at[2, p], fr.at[2, p], mate)

    def deliver(p):
        at = first(p, 1 - flip)
        src, dst = state.at[2 * ITERS, pl.ds(M + at, W), rows], out.at[0, pl.ds(at, W)]
        return remote(src, dst, fs.at[2, p], fr.at[2, p], across)

    def give(p):
        pl.when(shared(p))(lambda: pass_on(p, flip).start())
        pl.when(jnp.logical_not(shared(p)))(lambda: returned(p).start())

    def given(p):
        pl.when(shared(p))(lambda: pass_on(p, flip).wait_send())
        pl.when(jnp.logical_not(shared(p)))(lambda: returned(p).wait_send())

    def edge(src, dst, planes, slot, dev):
        near, beyond = (1 - flip) * (X - planes), M - planes + flip * (X + planes)
        src, dst = src.at[pl.ds(near, planes)], dst.at[pl.ds(beyond, planes), rows]
        return remote(src, dst, fs.at[3, slot], fr.at[3, slot], dev)

    base_edge = edge(fields.at[0], state.at[0], 2 * ITERS - 1, 0, mate)
    base_edge_across = edge(fields.at[0], state.at[0], 2 * ITERS - 1, 1, across)
    force_edge = edge(forcing, force, 2 * ITERS - 2, 2, mate)
    adjoint_edge = edge(fields.at[0], state.at[ITERS], ITERS, 3, mate)
    adjoint_edge_across = edge(fields.at[0], state.at[ITERS], ITERS, 4, across)

    def far_edge(src, dst, planes, slot):
        near, beyond = flip * (X - planes), M + X - flip * (X + planes)
        src, dst = src.at[pl.ds(near, planes)], dst.at[pl.ds(beyond, planes), rows]
        return remote(src, dst, fs.at[3, slot], fr.at[3, slot], far)

    own_base = state.at[0, pl.ds(M, X), rows]
    own_adjoint = state.at[ITERS, pl.ds(M, X), rows]
    base_far = far_edge(fields.at[0], state.at[0], 2 * ITERS - 1, 5)
    base_far_on = far_edge(own_base, state.at[0], 2 * ITERS - 1, 5)
    force_far = far_edge(forcing, force, 2 * ITERS - 2, 6)
    adjoint_far = far_edge(fields.at[0], state.at[ITERS], ITERS, 7)
    adjoint_far_on = far_edge(own_adjoint, state.at[ITERS], ITERS, 7)

    def send_y(k, p):
        pl.when(has_down)(lambda: y_down(k, p).start())
        pl.when(has_up)(lambda: y_up(k, p).start())

    def recv_y(k, p):
        pl.when(has_up)(lambda: y_down(k, p).wait_recv())
        pl.when(has_down)(lambda: y_up(k, p).wait_recv())

    force_in = pltpu.make_async_copy(forcing, force.at[pl.ds(M, X), rows], local.at[0])

    def own(k):
        return pltpu.make_async_copy(fields.at[0], state.at[k, pl.ds(M, X), rows], local.at[1])

    barrier = pltpu.get_barrier_semaphore()

    def greet(dev):
        pl.semaphore_signal(barrier, inc=1, device_id=dev, device_id_type=MESH)

    greet(other)
    greet(mate)
    greet(across)
    pl.when(has_far)(lambda: greet(far))
    pl.when(has_down)(lambda: greet(down))
    pl.when(has_up)(lambda: greet(up))
    pl.when(base_side)(lambda: own(0).start())
    pl.when(home_full)(lambda: own(ITERS).start())
    pl.when(works)(lambda: force_in.start())
    peers = 3 + has_far.astype(jnp.int32) + has_down.astype(jnp.int32) + has_up.astype(jnp.int32)
    pl.semaphore_wait(barrier, peers)

    @pl.when(base_only)
    def _():
        brick(0).start()
        base_edge.start()
        force_edge.start()

        @pl.when(has_far)
        def _():
            base_far.start()
            force_far.start()

        @pl.loop(1, n)
        def _(p):
            brick(p).start()

    @pl.when(away_full)
    def _():
        base_edge_across.start()

        @pl.when(has_far)
        def _():
            base_far.start()
            force_far.start()

        base_edge.start()
        force_edge.start()

    @pl.when(idle)
    def _():
        lent(0).start()
        adjoint_edge.start()
        force_edge.start()

        @pl.loop(1, n)
        def _(p):
            lent(p).start()

    @pl.when(home_full)
    def _():
        adjoint_edge_across.start()

        @pl.when(has_far)
        def _():
            adjoint_far.start()
            force_far.start()

    lane = lax.broadcasted_iota(jnp.int32, (R, Z), 1)
    low = jnp.broadcast_to(has_down, (H, Z))
    high = jnp.broadcast_to(has_up, (H, Z))

    def around(mid):
        below, above = pltpu.roll(mid, 1, 0), pltpu.roll(mid, R - 1, 0)
        before = jnp.where(lane == 0, 0.0, pltpu.roll(mid, 1, 1))
        after = jnp.where(lane == Z - 1, 0.0, pltpu.roll(mid, Z - 1, 1))
        return (below + above) + (before + after)

    def forward(k, p, put):
        scale = level[k, 0:1, :]
        for j in range(W):
            i = first(p) + j
            mid, prev, nxt = state[k, M + i], state[k, M + i - 1], state[k, M + i + 1]
            total = around(mid) + (nxt + prev) - mid * (nxt - prev)
            put(i, 0.4 * mid + 0.1 * total + force[M + i] * scale)

    def backward(k, b, p, put):
        for j in range(W):
            i = first(p) + j
            mid, prev, nxt = state[k, M + i], state[k, M + i - 1], state[k, M + i + 1]
            total = around(mid) + (nxt + prev)
            total = total + state[b, M + i + 1] * (nxt - mid) - state[b, M + i - 1] * (prev - mid)
            put(i, 0.4 * mid + 0.1 * total)

    def into_level(k):
        def put(i, value):
            state[k, M + i, 0:H] = jnp.where(low, value[0:H], 0.0)
            state[k, M + i, H : H + Y] = value[H : H + Y]
            state[k, M + i, H + Y : R] = jnp.where(high, value[H + Y : R], 0.0)

        return put

    def into_return(i, value):
        state[2 * ITERS, M + i, H : H + Y] = value[H : H + Y]

    def into_out(i, value):
        out[0, i] = value[H : H + Y]

    @pl.when(works)
    def _():
        for k in range(ITERS):
            phase = (step_ref[0] + k).astype(jnp.float32) * (2.0 * math.pi / 64.0)
            level[k] = 0.2 * jnp.sin(jnp.full((8, Z), phase, jnp.float32))

        @pl.loop(0, 2 * ITERS)
        def _(k):
            @pl.when(jnp.logical_not(has_far))
            def _():
                state[k, M - 1 + flip * (X + 1)] = jnp.zeros((R, Z), jnp.float32)

        def clear(at):
            @pl.loop(0, X + W)
            def _(i):
                state[0, M - flip * W + i, at] = jnp.zeros((H, Z), jnp.float32)
                state[ITERS, M - flip * W + i, at] = jnp.zeros((H, Z), jnp.float32)

        pl.when(jnp.logical_not(has_down))(lambda: clear(pl.ds(0, H)))
        pl.when(jnp.logical_not(has_up))(lambda: clear(pl.ds(H + Y, H)))
        pl.when(base_side)(lambda: own(0).wait())
        pl.when(home_full)(lambda: own(ITERS).wait())
        force_in.wait()

        def ahead(p):
            pl.when(base_side)(lambda: send_y(0, p))
            send_y(2, p)
            pl.when(home_full)(lambda: send_y(1, p))

        pl.loop(0, AHEAD)(ahead)

        def begin(p):
            pl.when(jnp.logical_and(home_full, p < n))(lambda: brick(p).wait_recv())
            pl.when(jnp.logical_and(jnp.logical_and(home_full, has_far), p == 0))(lambda: base_far_on.start())

            @pl.when(p == n)
            def _():
                pl.when(home_full)(lambda: base_edge_across.wait_recv())
                pl.when(base_side)(lambda: base_edge.wait_recv())
                force_edge.wait_recv()

            pl.when(jnp.logical_or(home_full, p == n))(lambda: send_y(0, p))
            pl.when(p == n)(lambda: send_y(2, p))

        def begin_far():
            base_far.wait_recv()
            force_far.wait_recv()
            send_y(0, -1)
            send_y(2, -1)

        def gather(p):
            recv_y(0, p)
            recv_y(2, p)

        def borrow(p):
            pl.when(jnp.logical_and(away_full, p < n))(lambda: lent(p).wait_recv())
            pl.when(jnp.logical_and(jnp.logical_and(away_full, has_far), p == 0))(lambda: adjoint_far_on.start())

            @pl.when(p == n)
            def _():
                pl.when(home_full)(lambda: adjoint_edge.wait_recv())
                pl.when(away_full)(lambda: adjoint_edge_across.wait_recv())

            pl.when(jnp.logical_or(away_full, p == n))(lambda: send_y(1, p))

        def borrow_far():
            adjoint_far.wait_recv()
            send_y(1, -1)

        def gather_adjoint(p):
            recv_y(1, p)

        def step_base(k, p):
            forward(k, p, into_level(k + 1))

        def last_base(p):
            forward(ITERS - 1, p, into_out)

        def step_adjoint(m, p):
            k, b = ITERS + m, ITERS - 1 - m
            backward(k, b, p, into_level(k + 1))

        def last_adjoint(p):
            k, b = 2 * ITERS - 1, 0
            pl.when(home_full)(lambda: backward(k, b, p, into_out))
            pl.when(away_full)(lambda: backward(k, b, p, into_return))

        lowest = -has_far.astype(jnp.int32)
        full_far = jnp.logical_and(is_full, has_far)

        def task(p, hi, run, extra=None, lo=0):
            ok = jnp.logical_and(p >= lo, p < hi)
            pl.when(ok if extra is None else jnp.logical_and(ok, extra))(functools.partial(run, p))

        @pl.loop(0, n + 2 * ITERS + 1)
        def _(t):
            pl.when(t + AHEAD < n)(lambda: ahead(t + AHEAD))
            task(t, n + 1, begin)
            pl.when(jnp.logical_and(has_far, t == 1))(begin_far)
            task(t - 2, n + 1, gather)
            pl.when(jnp.logical_and(has_far, t == 2))(lambda: gather(-1))

            @pl.loop(0, ITERS - 1)
            def _(k):
                task(t - 3 - k, n + 1, functools.partial(step_base, k), lo=lowest)

            task(t - ITERS, n + 1, borrow, is_full)
            pl.when(jnp.logical_and(full_far, t == ITERS))(borrow_far)
            task(t - ITERS - 1, n + 1, gather_adjoint, is_full)
            pl.when(jnp.logical_and(full_far, t == ITERS + 1))(lambda: gather_adjoint(-1))

            @pl.loop(0, ITERS - 1)
            def _(m):
                task(t - ITERS - 2 - m, n + 1, functools.partial(step_adjoint, m), is_full, lowest)

            task(t - 2 * ITERS - 1, n, last_adjoint, is_full)

            @pl.when(jnp.logical_and(away_full, t == hold))
            def _():
                pl.semaphore_wait(go, 1)

                @pl.loop(0, hold - 2 * ITERS)
                def _(p):
                    give(p)

            @pl.when(jnp.logical_and(away_full, t > hold))
            def _():
                give(t - 2 * ITERS - 1)

            task(t - ITERS - 2, n, last_base, base_side)

            @pl.when(jnp.logical_and(base_only, t == 7))
            def _():
                @pl.loop(0, n - EARLY)
                def _(p):
                    brick(p).wait_send()

                pl.semaphore_signal(go, inc=1, device_id=mate, device_id_type=MESH)

        def sent_y(k):
            @pl.loop(lowest, n + 1)
            def _(p):
                pl.when(has_down)(lambda: y_down(k, p).wait_send())
                pl.when(has_up)(lambda: y_up(k, p).wait_send())

        sent_y(0)
        sent_y(2)
        pl.when(is_full)(lambda: sent_y(1))

        @pl.when(has_far)
        def _():
            base_far.wait_send()
            force_far.wait_send()
            pl.when(is_full)(lambda: adjoint_far.wait_send())

    @pl.when(base_only)
    def _():
        @pl.loop(FROM, n)
        def _(p):
            @pl.when(shared(p))
            def _():
                pass_on(p, 1 - flip).wait_recv()
                deliver(p).start()

        @pl.loop(FROM, n)
        def _(p):
            pl.when(shared(p))(lambda: deliver(p).wait_send())

        @pl.loop(n - EARLY, n)
        def _(p):
            brick(p).wait_send()

        base_edge.wait_send()
        force_edge.wait_send()

    @pl.when(away_full)
    def _():
        base_edge_across.wait_send()
        base_edge.wait_send()
        force_edge.wait_send()

        pl.loop(0, n)(given)

    @pl.when(home_full)
    def _():
        adjoint_edge_across.wait_send()

    @pl.when(idle)
    def _():

        @pl.loop(0, n)
        def _(p):
            lent(p).wait_send()

        adjoint_edge.wait_send()
        force_edge.wait_send()

        @pl.loop(0, n)
        def _(p):
            returned(p).wait_recv()


def on_device(fields, forcing, step_index):
    X, Y, Z = forcing.shape
    W = H = 8
    n = X // W
    assert X % W == 0 and lax.axis_size("gx") % 2 == 0 and W >= 2 * ITERS - 1 and Y >= 2 * H
    levels = 2 * ITERS
    planes = X + 2 * W + 2
    return pl.pallas_call(
        functools.partial(window, W, H),
        out_shape=pltpu.VMEM(fields.shape, jnp.float32),
        in_specs=[pl.BlockSpec(memory_space=pltpu.SMEM)] + [pl.BlockSpec(memory_space=pltpu.HBM)] * 2,
        out_specs=pl.BlockSpec(memory_space=pltpu.VMEM),
        scratch_shapes=[
            pltpu.VMEM((levels + 1, planes, Y + 2 * H, Z), jnp.float32),
            pltpu.VMEM((planes, Y + 2 * H, Z), jnp.float32),
            pltpu.VMEM((ITERS, 8, Z), jnp.float32),
            pltpu.SemaphoreType.DMA((3, 2, n + 2)),
            pltpu.SemaphoreType.DMA((3, 2, n + 2)),
            pltpu.SemaphoreType.DMA((4, max(n, 8))),
            pltpu.SemaphoreType.DMA((4, max(n, 8))),
            pltpu.SemaphoreType.DMA((2,)),
            pltpu.SemaphoreType.REGULAR,
        ],
        compiler_params=pltpu.CompilerParams(
            collective_id=0, has_side_effects=True, vmem_limit_bytes=48 * 1024 * 1024
        ),
        name="window",
    )(step_index, *(pltpu.with_memory_space_constraint(a, pltpu.HBM) for a in (fields, forcing)))


def solution(mesh):
    placed = (P("half", "gx", "yz", None), P("gx", "yz", None), P())
    return jax.shard_map(
        on_device,
        mesh=mesh,
        in_specs=placed,
        out_specs=P("half", "gx", "yz", None),
        check_vma=False,
    )
```

```python
import functools
import math

import jax
import jax.numpy as jnp
from jax import lax
from jax.experimental import pallas as pl
from jax.experimental.pallas import tpu as pltpu
from jax.sharding import PartitionSpec as P

ITERS = 4
EARLY = 3
AHEAD = 2
FROM = 3
MESH = pl.DeviceIdType.MESH


def window(W, H, step_ref, fields, forcing, out, state, force, level, ys, yr, fs, fr, local, go):
    X, Y, Z = forcing.shape
    n = X // W
    M = W + 1
    R = Y + 2 * H
    rows = pl.ds(H, Y)
    hold = n + 1
    side = lax.axis_index("half")
    gx, nx = lax.axis_index("gx"), lax.axis_size("gx")
    gy, ny = lax.axis_index("yz"), lax.axis_size("yz")

    flip = lax.rem(gx, 2)
    home = lax.rem(lax.div(gx + 1, 2), 2)
    full = jnp.where(side == 1, home, 1 - home)
    base_side = side == 0
    is_full, is_home = full == 1, home == 1
    works = jnp.logical_or(base_side, is_full)
    away_full = jnp.logical_and(base_side, is_full)
    home_full = jnp.logical_and(side == 1, is_full)
    base_only = jnp.logical_and(base_side, is_home)
    idle = jnp.logical_and(side == 1, home == 0)

    has_far = jnp.logical_or(jnp.logical_and(flip == 0, gx > 0), jnp.logical_and(flip == 1, gx < nx - 1))
    has_down, has_up = gy > 0, gy < ny - 1
    far = {"gx": lax.rem(gx + nx - 1 + 2 * flip, nx)}
    mate = {"gx": gx + 1 - 2 * flip}
    down, up = {"yz": lax.rem(gy + ny - 1, ny)}, {"yz": lax.rem(gy + 1, ny)}
    other = {"half": 1 - side}
    across = {"half": 1 - side, "gx": gx + 1 - 2 * flip}

    def first(p, flip=flip):
        return p * W + flip * (X - (2 * p + 1) * W)

    def shared(p):
        return jnp.logical_and(p >= FROM, lax.rem(p - FROM, 2) == 0)

    def remote(src, dst, s, r, dev):
        return pltpu.make_async_remote_copy(
            src_ref=src, dst_ref=dst, send_sem=s, recv_sem=r, device_id=dev, device_id_type=MESH
        )

    sources = (state.at[0], state.at[ITERS], force)

    def y_down(k, p):
        src = sources[k].at[pl.ds(M + first(p), W)]
        return remote(src.at[:, pl.ds(H, H)], src.at[:, pl.ds(H + Y, H)], ys.at[k, 0, p + 1], yr.at[k, 0, p + 1], down)

    def y_up(k, p):
        src = sources[k].at[pl.ds(M + first(p), W)]
        return remote(src.at[:, pl.ds(Y, H)], src.at[:, pl.ds(0, H)], ys.at[k, 1, p + 1], yr.at[k, 1, p + 1], up)

    def brick(p):
        src, dst = fields.at[0, pl.ds(first(p), W)], state.at[0, pl.ds(M + first(p), W), rows]
        return remote(src, dst, fs.at[0, p], fr.at[0, p], other)

    def lent(p):
        src, dst = fields.at[0, pl.ds(first(p), W)], state.at[ITERS, pl.ds(M + first(p), W), rows]
        return remote(src, dst, fs.at[1, p], fr.at[1, p], other)

    def returned(p):
        src, dst = state.at[2 * ITERS, pl.ds(M + first(p), W), rows], out.at[0, pl.ds(first(p), W)]
        return remote(src, dst, fs.at[2, p], fr.at[2, p], other)

    def pass_on(p, flip):
        part = state.at[2 * ITERS, pl.ds(M + first(p, flip), W), rows]
        return remote(part, part, fs.at[2, p], fr.at[2, p], mate)

    def deliver(p):
        at = first(p, 1 - flip)
        src, dst = state.at[2 * ITERS, pl.ds(M + at, W), rows], out.at[0, pl.ds(at, W)]
        return remote(src, dst, fs.at[2, p], fr.at[2, p], across)

    def give(p):
        pl.when(shared(p))(lambda: pass_on(p, flip).start())
        pl.when(jnp.logical_not(shared(p)))(lambda: returned(p).start())

    def given(p):
        pl.when(shared(p))(lambda: pass_on(p, flip).wait_send())
        pl.when(jnp.logical_not(shared(p)))(lambda: returned(p).wait_send())

    def edge(src, dst, planes, slot, dev):
        near, beyond = (1 - flip) * (X - planes), M - planes + flip * (X + planes)
        src, dst = src.at[pl.ds(near, planes)], dst.at[pl.ds(beyond, planes), rows]
        return remote(src, dst, fs.at[3, slot], fr.at[3, slot], dev)

    base_edge = edge(fields.at[0], state.at[0], 2 * ITERS - 1, 0, mate)
    base_edge_across = edge(fields.at[0], state.at[0], 2 * ITERS - 1, 1, across)
    force_edge = edge(forcing, force, 2 * ITERS - 2, 2, mate)
    adjoint_edge = edge(fields.at[0], state.at[ITERS], ITERS, 3, mate)
    adjoint_edge_across = edge(fields.at[0], state.at[ITERS], ITERS, 4, across)

    def far_edge(src, dst, planes, slot):
        near, beyond = flip * (X - planes), M + X - flip * (X + planes)
        src, dst = src.at[pl.ds(near, planes)], dst.at[pl.ds(beyond, planes), rows]
        return remote(src, dst, fs.at[3, slot], fr.at[3, slot], far)

    own_base = state.at[0, pl.ds(M, X), rows]
    own_adjoint = state.at[ITERS, pl.ds(M, X), rows]
    base_far = far_edge(fields.at[0], state.at[0], 2 * ITERS - 1, 5)
    base_far_on = far_edge(own_base, state.at[0], 2 * ITERS - 1, 5)
    force_far = far_edge(forcing, force, 2 * ITERS - 2, 6)
    adjoint_far = far_edge(fields.at[0], state.at[ITERS], ITERS, 7)
    adjoint_far_on = far_edge(own_adjoint, state.at[ITERS], ITERS, 7)

    def send_y(k, p):
        pl.when(has_down)(lambda: y_down(k, p).start())
        pl.when(has_up)(lambda: y_up(k, p).start())

    def recv_y(k, p):
        pl.when(has_up)(lambda: y_down(k, p).wait_recv())
        pl.when(has_down)(lambda: y_up(k, p).wait_recv())

    force_in = pltpu.make_async_copy(forcing, force.at[pl.ds(M, X), rows], local.at[0])

    def own(k):
        return pltpu.make_async_copy(fields.at[0], state.at[k, pl.ds(M, X), rows], local.at[1])

    barrier = pltpu.get_barrier_semaphore()

    def greet(dev):
        pl.semaphore_signal(barrier, inc=1, device_id=dev, device_id_type=MESH)

    greet(other)
    greet(mate)
    greet(across)
    pl.when(has_far)(lambda: greet(far))
    pl.when(has_down)(lambda: greet(down))
    pl.when(has_up)(lambda: greet(up))
    pl.when(base_side)(lambda: own(0).start())
    pl.when(home_full)(lambda: own(ITERS).start())
    pl.when(works)(lambda: force_in.start())
    peers = 3 + has_far.astype(jnp.int32) + has_down.astype(jnp.int32) + has_up.astype(jnp.int32)
    pl.semaphore_wait(barrier, peers)

    @pl.when(base_only)
    def _():
        brick(0).start()
        base_edge.start()
        force_edge.start()

        @pl.when(has_far)
        def _():
            base_far.start()
            force_far.start()

        @pl.loop(1, n)
        def _(p):
            brick(p).start()

    @pl.when(away_full)
    def _():
        base_edge_across.start()

        @pl.when(has_far)
        def _():
            base_far.start()
            force_far.start()

        base_edge.start()
        force_edge.start()

    @pl.when(idle)
    def _():
        lent(0).start()
        adjoint_edge.start()
        force_edge.start()

        @pl.loop(1, n)
        def _(p):
            lent(p).start()

    @pl.when(home_full)
    def _():
        adjoint_edge_across.start()

        @pl.when(has_far)
        def _():
            adjoint_far.start()
            force_far.start()

    lane = lax.broadcasted_iota(jnp.int32, (R, Z), 1)
    low = jnp.broadcast_to(has_down, (H, Z))
    high = jnp.broadcast_to(has_up, (H, Z))

    def around(mid):
        below, above = pltpu.roll(mid, 1, 0), pltpu.roll(mid, R - 1, 0)
        before = jnp.where(lane == 0, 0.0, pltpu.roll(mid, 1, 1))
        after = jnp.where(lane == Z - 1, 0.0, pltpu.roll(mid, Z - 1, 1))
        return (below + above) + (before + after)

    def forward(k, p, put):
        scale = level[k, 0:1, :]
        for j in range(W):
            i = first(p) + j
            mid, prev, nxt = state[k, M + i], state[k, M + i - 1], state[k, M + i + 1]
            total = around(mid) + (nxt + prev) - mid * (nxt - prev)
            put(i, 0.4 * mid + 0.1 * total + force[M + i] * scale)

    def backward(k, b, p, put):
        for j in range(W):
            i = first(p) + j
            mid, prev, nxt = state[k, M + i], state[k, M + i - 1], state[k, M + i + 1]
            total = around(mid) + (nxt + prev)
            total = total + state[b, M + i + 1] * (nxt - mid) - state[b, M + i - 1] * (prev - mid)
            put(i, 0.4 * mid + 0.1 * total)

    def into_level(k):
        def put(i, value):
            state[k, M + i, 0:H] = jnp.where(low, value[0:H], 0.0)
            state[k, M + i, H : H + Y] = value[H : H + Y]
            state[k, M + i, H + Y : R] = jnp.where(high, value[H + Y : R], 0.0)

        return put

    def into_return(i, value):
        state[2 * ITERS, M + i, H : H + Y] = value[H : H + Y]

    def into_out(i, value):
        out[0, i] = value[H : H + Y]

    @pl.when(works)
    def _():
        for k in range(ITERS):
            phase = (step_ref[0] + k).astype(jnp.float32) * (2.0 * math.pi / 64.0)
            level[k] = 0.2 * jnp.sin(jnp.full((8, Z), phase, jnp.float32))

        @pl.loop(0, 2 * ITERS)
        def _(k):
            @pl.when(jnp.logical_not(has_far))
            def _():
                state[k, M - 1 + flip * (X + 1)] = jnp.zeros((R, Z), jnp.float32)

        def clear(at):
            @pl.loop(0, X + 2 * M)
            def _(i):
                state[0, i, at] = jnp.zeros((H, Z), jnp.float32)
                state[ITERS, i, at] = jnp.zeros((H, Z), jnp.float32)

        pl.when(jnp.logical_not(has_down))(lambda: clear(pl.ds(0, H)))
        pl.when(jnp.logical_not(has_up))(lambda: clear(pl.ds(H + Y, H)))
        pl.when(base_side)(lambda: own(0).wait())
        pl.when(home_full)(lambda: own(ITERS).wait())
        force_in.wait()

        def ahead(p):
            pl.when(base_side)(lambda: send_y(0, p))
            send_y(2, p)
            pl.when(home_full)(lambda: send_y(1, p))

        pl.loop(0, AHEAD)(ahead)

        def begin(p):
            pl.when(jnp.logical_and(home_full, p < n))(lambda: brick(p).wait_recv())
            pl.when(jnp.logical_and(jnp.logical_and(home_full, has_far), p == 0))(lambda: base_far_on.start())

            @pl.when(p == n)
            def _():
                pl.when(home_full)(lambda: base_edge_across.wait_recv())
                pl.when(base_side)(lambda: base_edge.wait_recv())
                force_edge.wait_recv()

            pl.when(jnp.logical_or(home_full, p == n))(lambda: send_y(0, p))
            pl.when(p == n)(lambda: send_y(2, p))

        def begin_far():
            base_far.wait_recv()
            force_far.wait_recv()
            send_y(0, -1)
            send_y(2, -1)

        def gather(p):
            recv_y(0, p)
            recv_y(2, p)

        def borrow(p):
            pl.when(jnp.logical_and(away_full, p < n))(lambda: lent(p).wait_recv())
            pl.when(jnp.logical_and(jnp.logical_and(away_full, has_far), p == 0))(lambda: adjoint_far_on.start())

            @pl.when(p == n)
            def _():
                pl.when(home_full)(lambda: adjoint_edge.wait_recv())
                pl.when(away_full)(lambda: adjoint_edge_across.wait_recv())

            pl.when(jnp.logical_or(away_full, p == n))(lambda: send_y(1, p))

        def borrow_far():
            adjoint_far.wait_recv()
            send_y(1, -1)

        def gather_adjoint(p):
            recv_y(1, p)

        def step_base(k, p):
            forward(k, p, into_level(k + 1))

        def last_base(p):
            forward(ITERS - 1, p, into_out)

        def step_adjoint(m, p):
            k, b = ITERS + m, ITERS - 1 - m
            backward(k, b, p, into_level(k + 1))

        def last_adjoint(p):
            k, b = 2 * ITERS - 1, 0
            pl.when(home_full)(lambda: backward(k, b, p, into_out))
            pl.when(away_full)(lambda: backward(k, b, p, into_return))

        lowest = -has_far.astype(jnp.int32)
        full_far = jnp.logical_and(is_full, has_far)

        def task(p, hi, run, extra=None, lo=0):
            ok = jnp.logical_and(p >= lo, p < hi)
            pl.when(ok if extra is None else jnp.logical_and(ok, extra))(functools.partial(run, p))

        @pl.loop(0, n + 2 * ITERS + 1)
        def _(t):
            pl.when(t + AHEAD < n)(lambda: ahead(t + AHEAD))
            task(t, n + 1, begin)
            pl.when(jnp.logical_and(has_far, t == 1))(begin_far)
            task(t - 2, n + 1, gather)
            pl.when(jnp.logical_and(has_far, t == 2))(lambda: gather(-1))

            @pl.loop(0, ITERS - 1)
            def _(k):
                task(t - 3 - k, n + 1, functools.partial(step_base, k), lo=lowest)

            task(t - ITERS, n + 1, borrow, is_full)
            pl.when(jnp.logical_and(full_far, t == ITERS))(borrow_far)
            task(t - ITERS - 1, n + 1, gather_adjoint, is_full)
            pl.when(jnp.logical_and(full_far, t == ITERS + 1))(lambda: gather_adjoint(-1))

            @pl.loop(0, ITERS - 1)
            def _(m):
                task(t - ITERS - 2 - m, n + 1, functools.partial(step_adjoint, m), is_full, lowest)

            task(t - 2 * ITERS - 1, n, last_adjoint, is_full)

            @pl.when(jnp.logical_and(away_full, t == hold))
            def _():
                pl.semaphore_wait(go, 1)

                @pl.loop(0, hold - 2 * ITERS)
                def _(p):
                    give(p)

            @pl.when(jnp.logical_and(away_full, t > hold))
            def _():
                give(t - 2 * ITERS - 1)

            task(t - ITERS - 2, n, last_base, base_side)

            @pl.when(jnp.logical_and(base_only, t == 7))
            def _():
                @pl.loop(0, n - EARLY)
                def _(p):
                    brick(p).wait_send()

                pl.semaphore_signal(go, inc=1, device_id=mate, device_id_type=MESH)

        def sent_y(k):
            @pl.loop(lowest, n + 1)
            def _(p):
                pl.when(has_down)(lambda: y_down(k, p).wait_send())
                pl.when(has_up)(lambda: y_up(k, p).wait_send())

        sent_y(0)
        sent_y(2)
        pl.when(is_full)(lambda: sent_y(1))

        @pl.when(has_far)
        def _():
            base_far.wait_send()
            force_far.wait_send()
            pl.when(is_full)(lambda: adjoint_far.wait_send())

    @pl.when(base_only)
    def _():
        @pl.loop(FROM, n)
        def _(p):
            @pl.when(shared(p))
            def _():
                pass_on(p, 1 - flip).wait_recv()
                deliver(p).start()

        @pl.loop(FROM, n)
        def _(p):
            pl.when(shared(p))(lambda: deliver(p).wait_send())

        @pl.loop(n - EARLY, n)
        def _(p):
            brick(p).wait_send()

        base_edge.wait_send()
        force_edge.wait_send()

    @pl.when(away_full)
    def _():
        base_edge_across.wait_send()
        base_edge.wait_send()
        force_edge.wait_send()

        pl.loop(0, n)(given)

    @pl.when(home_full)
    def _():
        adjoint_edge_across.wait_send()

    @pl.when(idle)
    def _():

        @pl.loop(0, n)
        def _(p):
            lent(p).wait_send()

        adjoint_edge.wait_send()
        force_edge.wait_send()

        @pl.loop(0, n)
        def _(p):
            returned(p).wait_recv()


def on_device(fields, forcing, step_index):
    X, Y, Z = forcing.shape
    W = H = 8
    n = X // W
    assert X % W == 0 and lax.axis_size("gx") % 2 == 0 and W >= 2 * ITERS - 1 and Y >= 2 * H
    levels = 2 * ITERS
    planes = X + 2 * W + 2
    return pl.pallas_call(
        functools.partial(window, W, H),
        out_shape=pltpu.VMEM(fields.shape, jnp.float32),
        in_specs=[pl.BlockSpec(memory_space=pltpu.SMEM)] + [pl.BlockSpec(memory_space=pltpu.HBM)] * 2,
        out_specs=pl.BlockSpec(memory_space=pltpu.VMEM),
        scratch_shapes=[
            pltpu.VMEM((levels + 1, planes, Y + 2 * H, Z), jnp.float32),
            pltpu.VMEM((planes, Y + 2 * H, Z), jnp.float32),
            pltpu.VMEM((ITERS, 8, Z), jnp.float32),
            pltpu.SemaphoreType.DMA((3, 2, n + 2)),
            pltpu.SemaphoreType.DMA((3, 2, n + 2)),
            pltpu.SemaphoreType.DMA((4, max(n, 8))),
            pltpu.SemaphoreType.DMA((4, max(n, 8))),
            pltpu.SemaphoreType.DMA((2,)),
            pltpu.SemaphoreType.REGULAR,
        ],
        compiler_params=pltpu.CompilerParams(
            collective_id=0, has_side_effects=True, vmem_limit_bytes=48 * 1024 * 1024
        ),
        name="window",
    )(step_index, *(pltpu.with_memory_space_constraint(a, pltpu.HBM) for a in (fields, forcing)))


def solution(mesh):
    placed = (P("half", "gx", "yz", None), P("gx", "yz", None), P())
    return jax.shard_map(
        on_device,
        mesh=mesh,
        in_specs=placed,
        out_specs=P("half", "gx", "yz", None),
        check_vma=False,
    )
```

```python
import functools
import math

import jax
import jax.numpy as jnp
from jax import lax
from jax.experimental import pallas as pl
from jax.experimental.pallas import tpu as pltpu
from jax.sharding import PartitionSpec as P

ITERS = 4
EARLY = 5
AHEAD = 2
FROM = 1
LAST = 1
MESH = pl.DeviceIdType.MESH


def window(W, H, step_ref, fields, forcing, out, state, passing, force, level, ys, yr, fs, fr, local, go):
    X, Y, Z = forcing.shape
    n = X // W
    M = W + 1
    R = Y + 2 * H
    rows = pl.ds(H, Y)
    hold = n + 1
    side = lax.axis_index("half")
    gx, nx = lax.axis_index("gx"), lax.axis_size("gx")
    gy, ny = lax.axis_index("yz"), lax.axis_size("yz")

    flip = lax.rem(gx, 2)
    home = lax.rem(lax.div(gx + 1, 2), 2)
    full = jnp.where(side == 1, home, 1 - home)
    base_side = side == 0
    is_full, is_home = full == 1, home == 1
    works = jnp.logical_or(base_side, is_full)
    away_full = jnp.logical_and(base_side, is_full)
    home_full = jnp.logical_and(side == 1, is_full)
    base_only = jnp.logical_and(base_side, is_home)
    idle = jnp.logical_and(side == 1, home == 0)

    has_far = jnp.logical_or(jnp.logical_and(flip == 0, gx > 0), jnp.logical_and(flip == 1, gx < nx - 1))
    has_down, has_up = gy > 0, gy < ny - 1
    far = {"gx": lax.rem(gx + nx - 1 + 2 * flip, nx)}
    mate = {"gx": gx + 1 - 2 * flip}
    down, up = {"yz": lax.rem(gy + ny - 1, ny)}, {"yz": lax.rem(gy + 1, ny)}
    other = {"half": 1 - side}
    across = {"half": 1 - side, "gx": gx + 1 - 2 * flip}

    def first(p, flip=flip):
        return p * W + flip * (X - (2 * p + 1) * W)

    def shared(p):
        return jnp.logical_and(p >= FROM, lax.rem(p - FROM, 2) == 0)

    def remote(src, dst, s, r, dev):
        return pltpu.make_async_remote_copy(
            src_ref=src, dst_ref=dst, send_sem=s, recv_sem=r, device_id=dev, device_id_type=MESH
        )

    sources = (state.at[0], state.at[ITERS], force)

    def y_down(k, p):
        src = sources[k].at[pl.ds(M + first(p), W)]
        return remote(src.at[:, pl.ds(H, H)], src.at[:, pl.ds(H + Y, H)], ys.at[k, 0, p + 1], yr.at[k, 0, p + 1], down)

    def y_up(k, p):
        src = sources[k].at[pl.ds(M + first(p), W)]
        return remote(src.at[:, pl.ds(Y, H)], src.at[:, pl.ds(0, H)], ys.at[k, 1, p + 1], yr.at[k, 1, p + 1], up)

    def brick(p):
        src, dst = fields.at[0, pl.ds(first(p), W)], state.at[0, pl.ds(M + first(p), W), rows]
        return remote(src, dst, fs.at[0, p], fr.at[0, p], other)

    def lent(p):
        src, dst = fields.at[0, pl.ds(first(p), W)], state.at[ITERS, pl.ds(M + first(p), W), rows]
        return remote(src, dst, fs.at[1, p], fr.at[1, p], other)

    def returned(p):
        src, dst = state.at[2 * ITERS, pl.ds(M + first(p), W), rows], out.at[0, pl.ds(first(p), W)]
        return remote(src, dst, fs.at[2, p], fr.at[2, p], other)

    def pass_on(p, flip):
        part = state.at[2 * ITERS, pl.ds(M + first(p, flip), W), rows]
        return remote(part, part, fs.at[2, p], fr.at[2, p], mate)

    def deliver(p):
        at = first(p, 1 - flip)
        src, dst = state.at[2 * ITERS, pl.ds(M + at, W), rows], out.at[0, pl.ds(at, W)]
        return remote(src, dst, fs.at[2, p], fr.at[2, p], across)

    def brick_aside(p):
        return remote(fields.at[0, pl.ds(first(p), W)], passing.at[p - 1], fs.at[0, p], fr.at[0, p], mate)

    def brick_onward(p):
        dst = state.at[0, pl.ds(M + first(p, 1 - flip), W), rows]
        return remote(passing.at[p - 1], dst, fs.at[0, p], fr.at[0, p], across)

    def give(p):
        pl.when(shared(p))(lambda: pass_on(p, flip).start())
        pl.when(jnp.logical_not(shared(p)))(lambda: returned(p).start())

    def given(p):
        pl.when(shared(p))(lambda: pass_on(p, flip).wait_send())
        pl.when(jnp.logical_not(shared(p)))(lambda: returned(p).wait_send())

    def edge(src, dst, planes, slot, dev):
        near, beyond = (1 - flip) * (X - planes), M - planes + flip * (X + planes)
        src, dst = src.at[pl.ds(near, planes)], dst.at[pl.ds(beyond, planes), rows]
        return remote(src, dst, fs.at[3, slot], fr.at[3, slot], dev)

    base_edge = edge(fields.at[0], state.at[0], 2 * ITERS - 1, 0, mate)
    base_edge_across = edge(fields.at[0], state.at[0], 2 * ITERS - 1, 1, across)
    force_edge = edge(forcing, force, 2 * ITERS - 2, 2, mate)
    adjoint_edge = edge(fields.at[0], state.at[ITERS], ITERS, 3, mate)
    adjoint_edge_across = edge(fields.at[0], state.at[ITERS], ITERS, 4, across)

    def far_edge(src, dst, planes, slot):
        near, beyond = flip * (X - planes), M + X - flip * (X + planes)
        src, dst = src.at[pl.ds(near, planes)], dst.at[pl.ds(beyond, planes), rows]
        return remote(src, dst, fs.at[3, slot], fr.at[3, slot], far)

    own_base = state.at[0, pl.ds(M, X), rows]
    own_adjoint = state.at[ITERS, pl.ds(M, X), rows]
    base_far = far_edge(fields.at[0], state.at[0], 2 * ITERS - 1, 5)
    base_far_on = far_edge(own_base, state.at[0], 2 * ITERS - 1, 5)
    force_far = far_edge(forcing, force, 2 * ITERS - 2, 6)
    adjoint_far = far_edge(fields.at[0], state.at[ITERS], ITERS, 7)
    adjoint_far_on = far_edge(own_adjoint, state.at[ITERS], ITERS, 7)

    def send_y(k, p):
        pl.when(has_down)(lambda: y_down(k, p).start())
        pl.when(has_up)(lambda: y_up(k, p).start())

    def recv_y(k, p):
        pl.when(has_up)(lambda: y_down(k, p).wait_recv())
        pl.when(has_down)(lambda: y_up(k, p).wait_recv())

    force_in = pltpu.make_async_copy(forcing, force.at[pl.ds(M, X), rows], local.at[0])

    def own(k):
        return pltpu.make_async_copy(fields.at[0], state.at[k, pl.ds(M, X), rows], local.at[1])

    barrier = pltpu.get_barrier_semaphore()

    def greet(dev):
        pl.semaphore_signal(barrier, inc=1, device_id=dev, device_id_type=MESH)

    greet(other)
    greet(mate)
    greet(across)
    pl.when(has_far)(lambda: greet(far))
    pl.when(has_down)(lambda: greet(down))
    pl.when(has_up)(lambda: greet(up))
    pl.when(base_side)(lambda: own(0).start())
    pl.when(home_full)(lambda: own(ITERS).start())
    pl.when(works)(lambda: force_in.start())
    peers = 3 + has_far.astype(jnp.int32) + has_down.astype(jnp.int32) + has_up.astype(jnp.int32)
    pl.semaphore_wait(barrier, peers)

    @pl.when(base_only)
    def _():
        brick(0).start()
        base_edge.start()
        force_edge.start()

        @pl.when(has_far)
        def _():
            base_far.start()
            force_far.start()

        pl.loop(1, LAST + 1)(lambda p: brick_aside(p).start())
        pl.loop(LAST + 1, n)(lambda p: brick(p).start())

    @pl.when(away_full)
    def _():
        base_edge_across.start()

        @pl.when(has_far)
        def _():
            base_far.start()
            force_far.start()

        base_edge.start()
        force_edge.start()

    @pl.when(idle)
    def _():
        lent(0).start()
        adjoint_edge.start()
        force_edge.start()

        @pl.loop(1, n)
        def _(p):
            lent(p).start()

    @pl.when(home_full)
    def _():
        adjoint_edge_across.start()

        @pl.when(has_far)
        def _():
            adjoint_far.start()
            force_far.start()

    lane = lax.broadcasted_iota(jnp.int32, (R, Z), 1)
    low = jnp.broadcast_to(has_down, (H, Z))
    high = jnp.broadcast_to(has_up, (H, Z))

    def around(mid):
        below, above = pltpu.roll(mid, 1, 0), pltpu.roll(mid, R - 1, 0)
        before = jnp.where(lane == 0, 0.0, pltpu.roll(mid, 1, 1))
        after = jnp.where(lane == Z - 1, 0.0, pltpu.roll(mid, Z - 1, 1))
        return (below + above) + (before + after)

    def forward(k, p, put):
        scale = level[k, 0:1, :]
        for j in range(W):
            i = first(p) + j
            mid, prev, nxt = state[k, M + i], state[k, M + i - 1], state[k, M + i + 1]
            total = around(mid) + (nxt + prev) - mid * (nxt - prev)
            put(i, 0.4 * mid + 0.1 * total + force[M + i] * scale)

    def backward(k, b, p, put):
        for j in range(W):
            i = first(p) + j
            mid, prev, nxt = state[k, M + i], state[k, M + i - 1], state[k, M + i + 1]
            total = around(mid) + (nxt + prev)
            total = total + state[b, M + i + 1] * (nxt - mid) - state[b, M + i - 1] * (prev - mid)
            put(i, 0.4 * mid + 0.1 * total)

    def into_level(k):
        def put(i, value):
            state[k, M + i, 0:H] = jnp.where(low, value[0:H], 0.0)
            state[k, M + i, H : H + Y] = value[H : H + Y]
            state[k, M + i, H + Y : R] = jnp.where(high, value[H + Y : R], 0.0)

        return put

    def into_return(i, value):
        state[2 * ITERS, M + i, H : H + Y] = value[H : H + Y]

    def into_out(i, value):
        out[0, i] = value[H : H + Y]

    @pl.when(works)
    def _():
        for k in range(ITERS):
            phase = (step_ref[0] + k).astype(jnp.float32) * (2.0 * math.pi / 64.0)
            level[k] = 0.2 * jnp.sin(jnp.full((8, Z), phase, jnp.float32))

        @pl.loop(0, 2 * ITERS)
        def _(k):
            @pl.when(jnp.logical_not(has_far))
            def _():
                state[k, M - 1 + flip * (X + 1)] = jnp.zeros((R, Z), jnp.float32)

        def clear(at):
            @pl.loop(0, X + 2 * M)
            def _(i):
                state[0, i, at] = jnp.zeros((H, Z), jnp.float32)
                state[ITERS, i, at] = jnp.zeros((H, Z), jnp.float32)

        pl.when(jnp.logical_not(has_down))(lambda: clear(pl.ds(0, H)))
        pl.when(jnp.logical_not(has_up))(lambda: clear(pl.ds(H + Y, H)))
        @pl.when(away_full)
        def _():
            @pl.loop(1, LAST + 1)
            def _(p):
                brick_aside(p).wait_recv()
                brick_onward(p).start()

        pl.when(base_side)(lambda: own(0).wait())
        pl.when(home_full)(lambda: own(ITERS).wait())
        force_in.wait()

        def ahead(p):
            pl.when(base_side)(lambda: send_y(0, p))
            send_y(2, p)
            pl.when(home_full)(lambda: send_y(1, p))

        pl.loop(0, AHEAD)(ahead)

        def begin(p):
            pl.when(jnp.logical_and(home_full, p < n))(lambda: brick(p).wait_recv())
            pl.when(jnp.logical_and(jnp.logical_and(home_full, has_far), p == 0))(lambda: base_far_on.start())

            @pl.when(p == n)
            def _():
                pl.when(home_full)(lambda: base_edge_across.wait_recv())
                pl.when(base_side)(lambda: base_edge.wait_recv())
                force_edge.wait_recv()

            pl.when(jnp.logical_or(home_full, p == n))(lambda: send_y(0, p))
            pl.when(p == n)(lambda: send_y(2, p))

        def begin_far():
            base_far.wait_recv()
            force_far.wait_recv()
            send_y(0, -1)
            send_y(2, -1)

        def gather(p):
            recv_y(0, p)
            recv_y(2, p)

        def borrow(p):
            pl.when(jnp.logical_and(away_full, p < n))(lambda: lent(p).wait_recv())
            pl.when(jnp.logical_and(jnp.logical_and(away_full, has_far), p == 0))(lambda: adjoint_far_on.start())

            @pl.when(p == n)
            def _():
                pl.when(home_full)(lambda: adjoint_edge.wait_recv())
                pl.when(away_full)(lambda: adjoint_edge_across.wait_recv())

            pl.when(jnp.logical_or(away_full, p == n))(lambda: send_y(1, p))

        def borrow_far():
            adjoint_far.wait_recv()
            send_y(1, -1)

        def gather_adjoint(p):
            recv_y(1, p)

        def step_base(k, p):
            forward(k, p, into_level(k + 1))

        def last_base(p):
            forward(ITERS - 1, p, into_out)

        def step_adjoint(m, p):
            k, b = ITERS + m, ITERS - 1 - m
            backward(k, b, p, into_level(k + 1))

        def last_adjoint(p):
            k, b = 2 * ITERS - 1, 0
            pl.when(home_full)(lambda: backward(k, b, p, into_out))
            pl.when(away_full)(lambda: backward(k, b, p, into_return))

        lowest = -has_far.astype(jnp.int32)
        full_far = jnp.logical_and(is_full, has_far)

        def task(p, hi, run, extra=None, lo=0):
            ok = jnp.logical_and(p >= lo, p < hi)
            pl.when(ok if extra is None else jnp.logical_and(ok, extra))(functools.partial(run, p))

        @pl.loop(0, n + 2 * ITERS + 1)
        def _(t):
            pl.when(t + AHEAD < n)(lambda: ahead(t + AHEAD))
            task(t, n + 1, begin)
            pl.when(jnp.logical_and(has_far, t == 1))(begin_far)
            task(t - 2, n + 1, gather)
            pl.when(jnp.logical_and(has_far, t == 2))(lambda: gather(-1))

            @pl.loop(0, ITERS - 1)
            def _(k):
                task(t - 3 - k, n + 1, functools.partial(step_base, k), lo=lowest)

            task(t - ITERS, n + 1, borrow, is_full)
            pl.when(jnp.logical_and(full_far, t == ITERS))(borrow_far)
            task(t - ITERS - 1, n + 1, gather_adjoint, is_full)
            pl.when(jnp.logical_and(full_far, t == ITERS + 1))(lambda: gather_adjoint(-1))

            @pl.loop(0, ITERS - 1)
            def _(m):
                task(t - ITERS - 2 - m, n + 1, functools.partial(step_adjoint, m), is_full, lowest)

            task(t - 2 * ITERS - 1, n, last_adjoint, is_full)

            @pl.when(jnp.logical_and(away_full, t == hold))
            def _():
                pl.semaphore_wait(go, 1)

                @pl.loop(0, hold - 2 * ITERS)
                def _(p):
                    give(p)

            @pl.when(jnp.logical_and(away_full, t > hold))
            def _():
                give(t - 2 * ITERS - 1)

            task(t - ITERS - 2, n, last_base, base_side)

            @pl.when(jnp.logical_and(base_only, t == 7))
            def _():
                pl.loop(1, LAST + 1)(lambda p: brick_aside(p).wait_send())
                brick(0).wait_send()
                pl.loop(LAST + 1, n - EARLY)(lambda p: brick(p).wait_send())

                pl.semaphore_signal(go, inc=1, device_id=mate, device_id_type=MESH)

        def sent_y(k):
            @pl.loop(lowest, n + 1)
            def _(p):
                pl.when(has_down)(lambda: y_down(k, p).wait_send())
                pl.when(has_up)(lambda: y_up(k, p).wait_send())

        sent_y(0)
        sent_y(2)
        pl.when(is_full)(lambda: sent_y(1))

        @pl.when(has_far)
        def _():
            base_far.wait_send()
            force_far.wait_send()
            pl.when(is_full)(lambda: adjoint_far.wait_send())

    @pl.when(base_only)
    def _():
        @pl.loop(FROM, n)
        def _(p):
            @pl.when(shared(p))
            def _():
                pass_on(p, 1 - flip).wait_recv()
                deliver(p).start()

        @pl.loop(FROM, n)
        def _(p):
            pl.when(shared(p))(lambda: deliver(p).wait_send())

        @pl.loop(n - EARLY, n)
        def _(p):
            brick(p).wait_send()

        base_edge.wait_send()
        force_edge.wait_send()

    @pl.when(away_full)
    def _():
        base_edge_across.wait_send()
        base_edge.wait_send()
        force_edge.wait_send()

        pl.loop(0, n)(given)
        pl.loop(1, LAST + 1)(lambda p: brick_onward(p).wait_send())

    @pl.when(home_full)
    def _():
        adjoint_edge_across.wait_send()

    @pl.when(idle)
    def _():

        @pl.loop(0, n)
        def _(p):
            lent(p).wait_send()

        adjoint_edge.wait_send()
        force_edge.wait_send()

        @pl.loop(0, n)
        def _(p):
            returned(p).wait_recv()


def on_device(fields, forcing, step_index):
    X, Y, Z = forcing.shape
    W = H = 8
    n = X // W
    assert X % W == 0 and lax.axis_size("gx") % 2 == 0 and W >= 2 * ITERS - 1 and Y >= 2 * H
    levels = 2 * ITERS
    planes = X + 2 * W + 2
    return pl.pallas_call(
        functools.partial(window, W, H),
        out_shape=pltpu.VMEM(fields.shape, jnp.float32),
        in_specs=[pl.BlockSpec(memory_space=pltpu.SMEM)] + [pl.BlockSpec(memory_space=pltpu.HBM)] * 2,
        out_specs=pl.BlockSpec(memory_space=pltpu.VMEM),
        scratch_shapes=[
            pltpu.VMEM((levels + 1, planes, Y + 2 * H, Z), jnp.float32),
            pltpu.VMEM((LAST, W, Y, Z), jnp.float32),
            pltpu.VMEM((planes, Y + 2 * H, Z), jnp.float32),
            pltpu.VMEM((ITERS, 8, Z), jnp.float32),
            pltpu.SemaphoreType.DMA((3, 2, n + 2)),
            pltpu.SemaphoreType.DMA((3, 2, n + 2)),
            pltpu.SemaphoreType.DMA((4, max(n, 8))),
            pltpu.SemaphoreType.DMA((4, max(n, 8))),
            pltpu.SemaphoreType.DMA((2,)),
            pltpu.SemaphoreType.REGULAR,
        ],
        compiler_params=pltpu.CompilerParams(
            collective_id=0, has_side_effects=True, vmem_limit_bytes=48 * 1024 * 1024
        ),
        name="window",
    )(step_index, *(pltpu.with_memory_space_constraint(a, pltpu.HBM) for a in (fields, forcing)))


def solution(mesh):
    placed = (P("half", "gx", "yz", None), P("gx", "yz", None), P())
    return jax.shard_map(
        on_device,
        mesh=mesh,
        in_specs=placed,
        out_specs=P("half", "gx", "yz", None),
        check_vma=False,
    )
```
